128 devices in a mesh: dp: 8 (over y, core), seq: 16 (over z, x).
Axes of the slice: x: 4, y: 4, z: 4, core: 2. Of those that a mesh axis runs over, the one named last changes fastest.
Arguments:
- loader_rows: bfloat16 [8, 8192, 1152], P('dp', 'seq'), may hold values from -6 to 6
- lengths: int32 [8, 128], P('dp'), may hold values from 1 to 128, 8192 in all within a row
- block_order: int32 [8, 64], P('dp'), may hold values from 0 to 63, as said below
- norm_gain: float32 [1152], replicated, may hold values from 0.1 to 1.9
- qkv_weight: bfloat16 [1152, 3456], replicated, may hold values from -0.1875 to 0.1875
- upstream_grad: bfloat16 [8, 8192, 1152], P('dp', 'seq'), may hold values from -6 to 6
Outputs:
- attention: bfloat16 [8, 8192, 1152], P('dp', 'seq')
- loader_grad: bfloat16 [8, 8192, 1152], P('dp', 'seq')
- weight_grad: float32 [1152, 3456], P('seq')
- gain_grad: float32 [1152], P('seq')
The draws below stay inside these ranges and needn't reach their ends.
Inputs may be any that keep to these rules, and one draw needn't show every extreme that they name: Images lie back to back in pack order; each pack's lengths sum to 8192. Each row of block_order is a permutation of the pack's 64 blocks. Of the blocks that one index of seq holds in pack order (blocks k * 4 onwards), no two come from the loader rows of the same index of seq, and no two loader blocks of one index of seq go to the same index.
All inputs are finite; a program needn't handle non-finite values.
Results may differ from the reference program's by a relative error of at most 0.015.
Values may be sent and summed in bfloat16 or wider, within the bound.
No kernel may reach another device: no remote copies, remote signals or barrier semaphores. Data moves between devices by JAX's collectives and lax.ppermute only.
A program may use at most 192 MiB of HBM per device.

```python
import math
import jax
import jax.numpy as jnp
import numpy as np
from jax import lax

HEADS = 16
HD = 72
D = 1152
TOK_DEV = 512
BLK = 128
L_MAX = 128
PACKS = 8
TOKENS = 8192
NBLK = 64
NIMG = 128
N_SEQ = 16


def draw_block_order(key, part):
    per_device = TOK_DEV // BLK
    device_count = NBLK // per_device

    def single_pack(pack_key):
        key_outer, key_inner, key_offset, key_turn = jax.random.split(pack_key, 4)
        outer_order = jax.random.permutation(key_outer, device_count).astype(jnp.int32)
        inner_order = jax.random.permutation(key_inner, device_count).astype(jnp.int32)
        offsets = jax.random.permutation(key_offset, device_count)[:per_device].astype(jnp.int32)
        slot_turns = jax.random.randint(key_turn, (device_count,), 0, per_device, dtype=jnp.int32)
        source = jnp.repeat(jnp.arange(device_count, dtype=jnp.int32), per_device)
        loader_slot = jnp.tile(jnp.arange(per_device, dtype=jnp.int32), device_count)
        target = outer_order[(inner_order[source] + offsets[loader_slot]) % device_count]
        target_slot = (loader_slot + slot_turns[target]) % per_device
        placed = target * per_device + target_slot
        return jnp.zeros((NBLK,), jnp.int32).at[placed].set(jnp.arange(NBLK, dtype=jnp.int32))
    return jax.vmap(single_pack)(jax.random.split(key, PACKS))


def block_levels(own_key, extent, cuts, smallest, high):
    level, own = 1.0, jax.random.fold_in(own_key, 6)
    for dim, parts in cuts:
        steps = jnp.exp(jax.random.uniform(jax.random.fold_in(own, dim), (parts,), jnp.float32, smallest / len(cuts), high / len(cuts)))
        level = level * jnp.repeat(steps, extent[dim] // parts).reshape([-1 if axis == dim else 1 for axis in range(len(extent))])
    return level


def profile(count, total, bound, skew):
    loads = [(1 << 20) // math.isqrt(rank ** skew) + 1 for rank in range(2, count + 1)]
    spare, given = total - bound - (count - 1), [1] * (count - 1)
    while spare > 0:
        free = [i for i in range(count - 1) if given[i] < bound]
        mass, remaining = sum([loads[i] for i in free]), spare
        for i in free:
            more = min(bound - given[i], max(1, remaining * loads[i] // mass), spare)
            given[i] = given[i] + more
            spare = spare - more
    return np.array([bound] + given)


def ragged(key, amount, total, limit, lean):
    if amount == 2:
        one = jax.random.randint(key, (), max(1, total - limit), min(limit, total - 1) + 1)
        return jnp.stack([one, total - one])
    tallies = jnp.asarray(profile(amount, total, limit, lean), jnp.int32)
    pairs = (amount - 1) // 2
    giver, receiver = tallies[1:1 + 2 * pairs:2], tallies[2:2 + 2 * pairs:2]
    margin = jnp.minimum(giver - 1, limit - receiver)
    shifted = jax.random.randint(jax.random.fold_in(key, 1), (pairs,), 0, 1 << 20) % (margin + 1)
    tallies = tallies.at[1:1 + 2 * pairs:2].set(giver - shifted).at[2:2 + 2 * pairs:2].set(receiver + shifted)
    return tallies[jax.random.permutation(jax.random.fold_in(key, 2), amount)]


def noise(key, dims, scale, bound, cuts=(), held_as=jnp.bfloat16):
    values = jax.random.normal(key, dims, jnp.float32) * scale
    if len(cuts) > 0:
        values = block_levels(key, dims, cuts, -0.22, 0.18) * values
    return jnp.clip(values, min=-bound, max=bound).astype(held_as)


def setup_inputs(seed: int = 0) -> dict:
    key_of = jax.random.split(jax.random.key(seed), 7)
    return {
        "loader_rows": noise(key_of[0], (PACKS, TOKENS, D), 1.0, 6.0, ((0, 8), (1, 16))),
        "lengths": jax.vmap(lambda own: ragged(own, NIMG, TOKENS, L_MAX, 2))(jax.random.split(key_of[1], PACKS)).reshape((PACKS, NIMG)).astype(jnp.int32),
        "block_order": draw_block_order(jax.random.fold_in(key_of[6], 71), 0),
        "norm_gain": jnp.clip(1.0 + 0.18 * jax.random.normal(key_of[3], (D,), jnp.float32), 0.1, 1.9),
        "qkv_weight": noise(key_of[4], (D, 3 * D), D ** -0.5, 0.1875),
        "upstream_grad": noise(key_of[5], (PACKS, TOKENS, D), 1.0, 6.0, ((0, 8), (1, 16))),
    }


epsilon = 1e-06

def image_ids(lengths, positions, row_total):
    image_ends = jnp.cumsum(lengths).astype(jnp.int32)
    counted = lax.optimization_barrier(jnp.sum((image_ends[None, :] <= positions[:, None]).astype(jnp.int32), axis=1)).astype(jnp.int32)
    inside = (positions >= 0) & (positions < row_total)
    return jnp.where(inside, counted, -1).astype(jnp.int32)

def one_pack(loader_rows, lengths, block_order, upstream_grad, norm_gain, qkv_weight):
    model_width = HEADS * HD
    score_scale = HD ** (-0.5)
    key_span = TOK_DEV + 2 * L_MAX
    pack_rows = jnp.take(loader_rows.reshape(NBLK, BLK, model_width), block_order, axis=0).reshape(TOKENS, model_width)
    values = pack_rows.astype(jnp.float32)
    centre = lax.optimization_barrier(jnp.mean(values, axis=1, keepdims=True))
    spread = lax.optimization_barrier(jnp.mean((values - centre) ** 2, axis=1, keepdims=True))
    inverse_std = lax.rsqrt(spread + epsilon)
    normed = (values - centre) * inverse_std
    scaled = (normed * norm_gain).astype(jnp.bfloat16)
    projected = jnp.dot(scaled, qkv_weight, preferred_element_type=jnp.float32).astype(jnp.bfloat16)
    projected = lax.optimization_barrier(projected).astype(jnp.float32)
    queries = projected[:, :model_width].reshape(TOKENS, HEADS, HD)
    padding = ((L_MAX, L_MAX), (0, 0), (0, 0))
    key_table = jnp.pad(projected[:, model_width:2 * model_width].reshape(TOKENS, HEADS, HD), padding)
    value_table = jnp.pad(projected[:, 2 * model_width:].reshape(TOKENS, HEADS, HD), padding)
    upstream = upstream_grad.astype(jnp.float32).reshape(TOKENS, HEADS, HD)
    positions = jnp.arange(-L_MAX, TOKENS + L_MAX, dtype=jnp.int32)
    key_ids = image_ids(lengths, positions, TOKENS)

    def block_step(totals, block_index):
        key_grads, value_grads = totals
        first_row = (block_index * TOK_DEV).astype(jnp.int32)
        query_block = lax.dynamic_slice_in_dim(queries, first_row, TOK_DEV, 0)
        upstream_block = lax.dynamic_slice_in_dim(upstream, first_row, TOK_DEV, 0)
        key_block = lax.dynamic_slice_in_dim(key_table, first_row, key_span, 0)
        value_block = lax.dynamic_slice_in_dim(value_table, first_row, key_span, 0)
        window_ids = lax.dynamic_slice_in_dim(key_ids, first_row, key_span, 0)
        query_ids = window_ids[L_MAX:L_MAX + TOK_DEV]
        visible = query_ids[:, None] == window_ids[None, :]
        scores = jnp.einsum('ihd,jhd->hij', query_block, key_block) * score_scale
        weights = jnp.where(visible[None], jnp.exp(scores), 0.0)
        probabilities = weights / lax.optimization_barrier(jnp.sum(weights, axis=2, keepdims=True))
        rounded = lax.optimization_barrier(probabilities.astype(jnp.bfloat16)).astype(jnp.float32)
        attended = jnp.einsum('hij,jhd->ihd', rounded, value_block)
        grad_probs = jnp.einsum('ihd,jhd->hij', upstream_block, value_block)
        centred = lax.optimization_barrier(jnp.sum(probabilities * grad_probs, axis=2, keepdims=True))
        grad_scores = (probabilities * (grad_probs - centred) * score_scale).astype(jnp.bfloat16)
        grad_scores = lax.optimization_barrier(grad_scores).astype(jnp.float32)
        query_grad = jnp.einsum('hij,jhd->ihd', grad_scores, key_block)
        key_part = jnp.einsum('hij,ihd->jhd', grad_scores, query_block)
        value_part = jnp.einsum('hij,ihd->jhd', rounded, upstream_block)
        key_grads = lax.dynamic_update_slice_in_dim(key_grads, lax.dynamic_slice_in_dim(key_grads, first_row, key_span, 0) + key_part, first_row, 0)
        value_grads = lax.dynamic_update_slice_in_dim(value_grads, lax.dynamic_slice_in_dim(value_grads, first_row, key_span, 0) + value_part, first_row, 0)
        return ((key_grads, value_grads), (attended.astype(jnp.bfloat16), query_grad))
    zero_table = jnp.zeros((TOKENS + 2 * L_MAX, HEADS, HD), jnp.float32)
    (key_grads, value_grads), (outputs, query_grads) = lax.scan(block_step, (zero_table, zero_table), jnp.arange(N_SEQ, dtype=jnp.int32))
    attention = outputs.reshape(TOKENS, model_width)
    grad_qkv = jnp.concatenate([query_grads.reshape(TOKENS, model_width), key_grads[L_MAX:L_MAX + TOKENS].reshape(TOKENS, model_width), value_grads[L_MAX:L_MAX + TOKENS].reshape(TOKENS, model_width)], axis=1).astype(jnp.bfloat16)
    weight_part = jnp.dot(scaled.T, grad_qkv, preferred_element_type=jnp.float32)
    input_grad = jnp.dot(grad_qkv, qkv_weight.T, preferred_element_type=jnp.float32)
    gain_part = lax.optimization_barrier(jnp.sum(input_grad * normed, axis=0))
    pushed = input_grad * norm_gain
    row_grad = inverse_std * (pushed - lax.optimization_barrier(jnp.mean(pushed, axis=1, keepdims=True)) - normed * lax.optimization_barrier(jnp.mean(pushed * normed, axis=1, keepdims=True)))
    grad_blocks = row_grad.astype(jnp.bfloat16).reshape(NBLK, BLK, model_width)
    loader_grad = jnp.zeros_like(grad_blocks).at[block_order].set(grad_blocks).reshape(TOKENS, model_width)
    return (attention, loader_grad, weight_part, gain_part)

def reference(loader_rows, lengths, block_order, norm_gain, qkv_weight, upstream_grad):

    def per_pack(pack_items):
        return one_pack(pack_items[0], pack_items[1], pack_items[2], pack_items[3], norm_gain, qkv_weight)
    attention, loader_grad, weight_parts, gain_parts = lax.map(per_pack, (loader_rows, lengths, block_order, upstream_grad))
    return (attention, loader_grad, lax.optimization_barrier(jnp.sum(weight_parts, axis=0)) / PACKS, lax.optimization_barrier(jnp.sum(gain_parts, axis=0)) / PACKS)
```

```python
import functools

import jax
import jax.numpy as jnp
from jax import lax
from jax.experimental import pallas as pl
from jax.experimental.pallas import tpu as pltpu
from jax.sharding import Mesh
from jax.sharding import PartitionSpec as P

HEADS = 16
HD = 72
BLK = 128
PAIR = 2 * HD
BF16 = jnp.bfloat16
F32 = jnp.float32
EPSILON = 1e-06
SCORE_SCALE = HD ** (-0.5)
HIDDEN_BIAS = -1e30
DP = ("y", "core")
SEQ = ("z", "x")


def nn(a, b):
    return lax.dot_general(a, b, (((1,), (0,)), ((), ())), preferred_element_type=F32)


def nt(a, b):
    return lax.dot_general(a, b, (((1,), (1,)), ((), ())), preferred_element_type=F32)


def attention_kernel(
    col_ref, row_ref, q_ref, k_ref, v_ref, qh_ref, kh_ref, vh_ref, g_ref, gh_ref,
    o_ref, dq_ref, dk_ref, dv_ref, bias_ref, o_s, dq_s, dk_s, dv_s,
):
    blocks = q_ref.shape[1] // BLK
    rows = q_ref.shape[1]

    @pl.when(pl.program_id(0) == 0)
    def _():
        for b in range(blocks + 2):
            first, last = max(b - 1, 0), min(b + 1, blocks + 1)
            same = col_ref[b * BLK : (b + 1) * BLK, :] == row_ref[:, first * BLK : (last + 1) * BLK]
            bias_ref[b, :, : (last + 1 - first) * BLK] = jnp.where(same, 0.0, HIDDEN_BIAS)

    for head in range(2):
        lo, hi = head * HD, (head + 1) * HD

        def whole(own, halo):
            mid, rim = own[...].astype(F32)[lo:hi], halo[...].astype(F32)[lo:hi]
            return jnp.concatenate([rim[:, :BLK], mid, rim[:, BLK:]], axis=1)

        q32, g32 = whole(q_ref, qh_ref), whole(g_ref, gh_ref)
        q, g = q32.astype(BF16), g32.astype(BF16)
        k, v = whole(k_ref, kh_ref).astype(BF16), whole(v_ref, vh_ref).astype(BF16)
        dk_s[lo:hi, :] = jnp.zeros((HD, rows), F32)
        dv_s[lo:hi, :] = jnp.zeros((HD, rows), F32)
        for b in range(blocks + 2):
            first, last = max(b - 1, 0), min(b + 1, blocks + 1)
            width = (last + 1 - first) * BLK
            k_win = k[:, first * BLK : (last + 1) * BLK]
            v_win = v[:, first * BLK : (last + 1) * BLK]
            here = slice(b * BLK, (b + 1) * BLK)
            scores = nn(q32[:, here].T.astype(BF16), k_win)
            grad_probs = nn(g32[:, here].T.astype(BF16), v_win)
            weights = jnp.exp(scores * SCORE_SCALE + bias_ref[b, :, :width])
            probs = weights * (1.0 / jnp.sum(weights, axis=1, keepdims=True))
            rounded = probs.astype(BF16)
            centred = jnp.sum(probs * grad_probs, axis=1, keepdims=True)
            grad_scores = (probs * (grad_probs - centred) * SCORE_SCALE).astype(BF16)
            if 1 <= b <= blocks:
                own = slice((b - 1) * BLK, b * BLK)
                o_s[lo:hi, own] = nt(v_win, rounded)
                dq_s[lo:hi, own] = nt(k_win, grad_scores)
            k0, k1 = max(first, 1), min(last, blocks)
            seen = slice((k0 - first) * BLK, (k1 + 1 - first) * BLK)
            into = slice((k0 - 1) * BLK, k1 * BLK)
            dk_s[lo:hi, into] += nn(q[:, here], grad_scores[:, seen])
            dv_s[lo:hi, into] += nn(g[:, here], rounded[:, seen])
    o_ref[...] = o_s[...].astype(BF16)
    dq_ref[...] = dq_s[...].astype(BF16)
    dk_ref[...] = dk_s[...].astype(BF16)
    dv_ref[...] = dv_s[...].astype(BF16)


def attention_call(ids, own, halo, g_own, g_halo, first_pair=0, pairs=HEADS // 2):
    rows, rim = own.shape[1], halo.shape[1]
    total, blocks = rows + rim, rows // BLK
    per_part = HEADS // 2

    def spec(width, part):
        return pl.BlockSpec((PAIR, width), lambda i: (part * per_part + first_pair + i, 0))

    out = pl.BlockSpec((PAIR, rows), lambda i: (i, 0))
    shape = jax.ShapeDtypeStruct((pairs * PAIR, rows), BF16)
    return pl.pallas_call(
        attention_kernel,
        grid=(pairs,),
        in_specs=[
            pl.BlockSpec((total, 1), lambda i: (0, 0)),
            pl.BlockSpec((1, total), lambda i: (0, 0)),
            spec(rows, 0), spec(rows, 1), spec(rows, 2),
            spec(rim, 0), spec(rim, 1), spec(rim, 2),
            spec(rows, 0), spec(rim, 0),
        ],
        out_specs=[out] * 4,
        out_shape=[shape] * 4,
        scratch_shapes=[pltpu.VMEM((blocks + 2, BLK, 3 * BLK), F32)]
        + [pltpu.VMEM((PAIR, rows), F32)] * 4,
        cost_estimate=pl.CostEstimate(
            flops=pairs * 2 * 16 * 12 * BLK * BLK * HD,
            bytes_accessed=pairs * PAIR * (rows * 8 + rim * 4) * 2,
            transcendentals=pairs * 2 * 16 * BLK * BLK,
        ),
        name="packed_attention",
    )(ids[:, None], ids[None, :], own, own, own, halo, halo, halo, g_own, g_halo)


def pick_kernel(index_ref, source_ref, out_ref):
    out_ref[...] = source_ref[...]


def pick(index, source):
    count, (_, rows, width) = index.shape[0], source.shape
    return pl.pallas_call(
        pick_kernel,
        grid_spec=pltpu.PrefetchScalarGridSpec(
            num_scalar_prefetch=1,
            grid=(count,),
            in_specs=[pl.BlockSpec((1, rows, width), lambda i, index: (index[i], 0, 0))],
            out_specs=pl.BlockSpec((1, rows, width), lambda i, index: (i, 0, 0)),
        ),
        out_shape=jax.ShapeDtypeStruct((count, rows, width), source.dtype),
        cost_estimate=pl.CostEstimate(
            flops=0, bytes_accessed=4 * count * rows * width, transcendentals=0
        ),
        name="pick_blocks",
    )(index, source)


def local(loader_rows, lengths, block_order, norm_gain, qkv_weight, upstream_grad):
    seq_count = lax.axis_size(SEQ)
    pack_count = lax.axis_size(DP)
    my_index = lax.axis_index(SEQ)
    _, row_count, model_width = loader_rows.shape
    per_device = row_count // BLK
    order_row = block_order[0]
    block_total = order_row.shape[0]
    devices = jnp.arange(seq_count, dtype=jnp.int32)
    slots = jnp.arange(per_device, dtype=jnp.int32)
    places = jnp.arange(block_total, dtype=jnp.int32)
    own_blocks = my_index * per_device + slots
    found = order_row[None, :] == own_blocks[:, None]
    target_device = jnp.sum(jnp.where(found, places[None, :], 0), axis=1) // per_device
    source_device = lax.dynamic_slice_in_dim(order_row, my_index * per_device, per_device) // per_device
    send_index = jnp.sum(jnp.where(devices[:, None] == target_device[None, :], slots[None, :], 0), axis=1)
    return_index = jnp.sum(jnp.where(devices[:, None] == source_device[None, :], slots[None, :], 0), axis=1)

    upstream = upstream_grad[0]
    up = [(i, i + 1) for i in range(seq_count - 1)]
    down = [(i + 1, i) for i in range(seq_count - 1)]

    def halo(x):
        before = lax.ppermute(x[row_count - BLK :], SEQ, up)
        after = lax.ppermute(x[:BLK], SEQ, down)
        return jnp.concatenate([before, after], axis=0)

    upstream_own = upstream.T
    upstream_halo = halo(upstream).T

    values = loader_rows[0].astype(F32)
    centre = jnp.mean(values, axis=1, keepdims=True)
    spread = jnp.mean((values - centre) ** 2, axis=1, keepdims=True)
    inverse_std = lax.rsqrt(spread + EPSILON)
    normed = (values - centre) * inverse_std
    scaled_loader = (normed * norm_gain).astype(BF16)

    outgoing = pick(send_index, scaled_loader.reshape(per_device, BLK, model_width))
    incoming = lax.all_to_all(outgoing, SEQ, split_axis=0, concat_axis=0, tiled=True)
    scaled = pick(source_device, incoming).reshape(row_count, model_width)
    scaled_halo = halo(scaled)

    def project(rows):
        return lax.dot_general(
            qkv_weight, rows, (((0,), (1,)), ((), ())), preferred_element_type=F32
        ).astype(BF16)

    qkv_own = project(scaled)
    qkv_halo = project(scaled_halo)
    image_ends = jnp.cumsum(lengths[0])
    positions = my_index * row_count - BLK + jnp.arange(row_count + 2 * BLK, dtype=jnp.int32)
    counted = jnp.sum((image_ends[None, :] <= positions[:, None]).astype(jnp.int32), axis=1)
    inside = (positions >= 0) & (positions < block_total * BLK)
    ids = jnp.where(inside, counted, -1)

    attended, query_grad, key_grad, value_grad = attention_call(
        ids, qkv_own, qkv_halo, upstream_own, upstream_halo
    )
    attention = attended.T[None]
    grad_cols = jnp.concatenate([query_grad, key_grad, value_grad], axis=0)
    weight_local = lax.dot_general(
        scaled, grad_cols, (((0,), (1,)), ((), ())), preferred_element_type=F32
    ).astype(BF16)
    input_grad = lax.dot_general(
        grad_cols, qkv_weight, (((0,), (1,)), ((), ())), preferred_element_type=F32
    ).astype(BF16)
    returning = pick(return_index, input_grad.reshape(per_device, BLK, model_width))
    returned = lax.all_to_all(returning, SEQ, split_axis=0, concat_axis=0, tiled=True)
    grads = pick(target_device, returned).reshape(row_count, model_width).astype(F32)
    pushed = grads * norm_gain
    row_grad = inverse_std * (
        pushed
        - jnp.mean(pushed, axis=1, keepdims=True)
        - normed * jnp.mean(pushed * normed, axis=1, keepdims=True)
    )
    loader_grad = row_grad.astype(BF16)[None]
    weight_share = lax.psum_scatter(weight_local, SEQ, scatter_dimension=0, tiled=True)
    weight_grad = lax.psum(weight_share, DP).astype(F32) / pack_count
    share = weight_grad.shape[0]
    weight_rows = lax.dynamic_slice_in_dim(qkv_weight, my_index * share, share, 0).astype(F32)
    gain_rows = lax.dynamic_slice_in_dim(norm_gain, my_index * share, share, 0)
    gain_grad = jnp.sum(weight_rows * weight_grad, axis=1) / gain_rows
    return (attention, loader_grad, weight_grad, gain_grad)


def solution(mesh):
    fine = Mesh(mesh.devices.reshape(4, 2, 4, 4), DP + SEQ)
    rows = P(DP, SEQ, None)
    return jax.shard_map(
        local,
        mesh=fine,
        in_specs=(rows, P(DP, None), P(DP, None), P(), P(), rows),
        out_specs=(rows, rows, P(SEQ, None), P(SEQ)),
        check_vma=False,
    )
```

```python
import functools

import jax
import jax.numpy as jnp
from jax import lax
from jax.experimental import pallas as pl
from jax.experimental.pallas import tpu as pltpu
from jax.sharding import Mesh
from jax.sharding import PartitionSpec as P

HEADS = 16
HD = 72
BLK = 128
PAIR = 2 * HD
BF16 = jnp.bfloat16
F32 = jnp.float32
EPSILON = 1e-06
SCORE_SCALE = HD ** (-0.5)
HIDDEN_BIAS = -1e30
DP = ("y", "core")
SEQ = ("z", "x")


def nn(a, b):
    return lax.dot_general(a, b, (((1,), (0,)), ((), ())), preferred_element_type=F32)


def nt(a, b):
    return lax.dot_general(a, b, (((1,), (1,)), ((), ())), preferred_element_type=F32)


def attention_kernel(
    col_ref, row_ref, q_ref, k_ref, v_ref, qh_ref, kh_ref, vh_ref, g_ref, gh_ref,
    o_ref, d_ref, bias_ref, o_s, d_s,
):
    blocks = q_ref.shape[1] // BLK
    rows = q_ref.shape[1]

    @pl.when(pl.program_id(0) == 0)
    def _():
        for b in range(blocks + 2):
            first, last = max(b - 1, 0), min(b + 1, blocks + 1)
            same = col_ref[b * BLK : (b + 1) * BLK, :] == row_ref[:, first * BLK : (last + 1) * BLK]
            bias_ref[b, :, : (last + 1 - first) * BLK] = jnp.where(same, 0.0, HIDDEN_BIAS)

    for head in range(2):
        lo, hi = head * HD, (head + 1) * HD

        def whole(own, halo):
            mid, rim = own[...].astype(F32)[lo:hi], halo[...].astype(F32)[lo:hi]
            return jnp.concatenate([rim[:, :BLK], mid, rim[:, BLK:]], axis=1)

        q32, g32 = whole(q_ref, qh_ref), whole(g_ref, gh_ref)
        q, g = q32.astype(BF16), g32.astype(BF16)
        k, v = whole(k_ref, kh_ref).astype(BF16), whole(v_ref, vh_ref).astype(BF16)
        q_at, k_at, v_at = (slice((3 * head + part) * HD, (3 * head + part + 1) * HD) for part in range(3))
        d_s[k_at, :] = jnp.zeros((HD, rows), F32)
        d_s[v_at, :] = jnp.zeros((HD, rows), F32)
        for b in range(blocks + 2):
            first, last = max(b - 1, 0), min(b + 1, blocks + 1)
            width = (last + 1 - first) * BLK
            k_win = k[:, first * BLK : (last + 1) * BLK]
            v_win = v[:, first * BLK : (last + 1) * BLK]
            here = slice(b * BLK, (b + 1) * BLK)
            scores = nn(q32[:, here].T.astype(BF16), k_win)
            grad_probs = nn(g32[:, here].T.astype(BF16), v_win)
            weights = jnp.exp(scores * SCORE_SCALE + bias_ref[b, :, :width])
            probs = weights * (1.0 / jnp.sum(weights, axis=1, keepdims=True))
            rounded = probs.astype(BF16)
            centred = jnp.sum(probs * grad_probs, axis=1, keepdims=True)
            grad_scores = (probs * (grad_probs - centred) * SCORE_SCALE).astype(BF16)
            if 1 <= b <= blocks:
                own = slice((b - 1) * BLK, b * BLK)
                o_s[lo:hi, own] = nt(v_win, rounded)
                d_s[q_at, own] = nt(k_win, grad_scores)
            k0, k1 = max(first, 1), min(last, blocks)
            seen = slice((k0 - first) * BLK, (k1 + 1 - first) * BLK)
            into = slice((k0 - 1) * BLK, k1 * BLK)
            d_s[k_at, into] += nn(q[:, here], grad_scores[:, seen])
            d_s[v_at, into] += nn(g[:, here], rounded[:, seen])
    o_ref[...] = o_s[...].astype(BF16)
    d_ref[...] = d_s[...].astype(BF16)


def attention_call(ids, own, halo, g_own, g_halo, first_pair=0, pairs=HEADS // 2):
    rows, rim = own.shape[1], halo.shape[1]
    total, blocks = rows + rim, rows // BLK
    per_part = HEADS // 2

    def spec(width, part):
        return pl.BlockSpec((PAIR, width), lambda i: (part * per_part + first_pair + i, 0))

    return pl.pallas_call(
        attention_kernel,
        grid=(pairs,),
        in_specs=[
            pl.BlockSpec((total, 1), lambda i: (0, 0)),
            pl.BlockSpec((1, total), lambda i: (0, 0)),
            spec(rows, 0), spec(rows, 1), spec(rows, 2),
            spec(rim, 0), spec(rim, 1), spec(rim, 2),
            spec(rows, 0), spec(rim, 0),
        ],
        out_specs=[
            pl.BlockSpec((PAIR, rows), lambda i: (i, 0)),
            pl.BlockSpec((3 * PAIR, rows), lambda i: (i, 0)),
        ],
        out_shape=[
            jax.ShapeDtypeStruct((pairs * PAIR, rows), BF16),
            jax.ShapeDtypeStruct((pairs * 3 * PAIR, rows), BF16),
        ],
        scratch_shapes=[
            pltpu.VMEM((blocks + 2, BLK, 3 * BLK), F32),
            pltpu.VMEM((PAIR, rows), F32),
            pltpu.VMEM((3 * PAIR, rows), F32),
        ],
        cost_estimate=pl.CostEstimate(
            flops=pairs * 2 * 16 * 12 * BLK * BLK * HD,
            bytes_accessed=pairs * PAIR * (rows * 8 + rim * 4) * 2,
            transcendentals=pairs * 2 * 16 * BLK * BLK,
        ),
        name="packed_attention",
    )(ids[:, None], ids[None, :], own, own, own, halo, halo, halo, g_own, g_halo)


def route_kernel(me_ref, order_ref, first_ref, cross_ref, last_ref, back_first_ref, back_cross_ref, back_last_ref, place, half, hue):
    me = me_ref[0]
    count = order_ref.shape[0]

    def clear(p, _):
        place[order_ref[p]] = p
        half[p] = -1
        hue[p] = -1
        return 0

    lax.fori_loop(0, count, clear, 0)

    def split(bits, partner, mate, seed):
        def start(i, _):
            def step(state):
                at, _ = state
                other = partner(at)
                bits[at] = 0
                bits[other] = 1
                following = mate(other)
                return following, bits[following] < 0

            at = seed(i)
            lax.while_loop(lambda state: state[1], step, (at, bits[at] < 0))
            return 0

        lax.fori_loop(0, count // 2, start, 0)

    split(half, lambda p: p ^ 1, lambda p: place[order_ref[p] ^ 1], lambda i: 2 * i)

    def same_half(p):
        return jnp.where(half[p ^ 2] == half[p], p ^ 2, p ^ 3)

    def same_half_loader(p):
        block = order_ref[p]
        near, far = place[block ^ 2], place[block ^ 3]
        return jnp.where(half[near] == half[p], near, far)

    split(hue, same_half, same_half_loader, lambda i: 4 * (i // 2) + i % 2)

    for slot in range(4):
        at = place[4 * me + slot]
        colour = 2 * half[at] + hue[at]
        first_ref[colour] = slot
        back_last_ref[slot] = colour
        at = 4 * me + slot
        colour = 2 * half[at] + hue[at]
        back_first_ref[colour] = slot
        last_ref[slot] = colour

    mine = me // 4

    def cross(p, _):
        @pl.when(2 * half[p] + hue[p] == mine)
        def _():
            source = order_ref[p] // 4
            cross_ref[p // 4] = source
            back_cross_ref[source] = p // 4

        return 0

    lax.fori_loop(0, count, cross, 0)


def route(me, order):
    smem = pl.BlockSpec(memory_space=pltpu.SMEM)
    sizes = (4, 16, 4, 4, 16, 4)
    return pl.pallas_call(
        route_kernel,
        in_specs=[smem, smem],
        out_specs=[smem] * len(sizes),
        out_shape=[jax.ShapeDtypeStruct((n,), jnp.int32) for n in sizes],
        scratch_shapes=[pltpu.SMEM(order.shape, jnp.int32)] * 3,
        name="route_blocks",
    )(me[None], order)


def pick_kernel(index_ref, source_ref, out_ref):
    for i in range(out_ref.shape[0]):
        out_ref[i] = source_ref[index_ref[i]]


def pick(index, source):
    shape = (index.shape[0],) + source.shape[1:]
    size = 2 * shape[0] * shape[1] * shape[2]
    return pl.pallas_call(
        pick_kernel,
        in_specs=[pl.BlockSpec(memory_space=pltpu.SMEM), pl.BlockSpec(memory_space=pltpu.VMEM)],
        out_specs=pl.BlockSpec(memory_space=pltpu.VMEM),
        out_shape=jax.ShapeDtypeStruct(shape, source.dtype),
        cost_estimate=pl.CostEstimate(flops=0, bytes_accessed=2 * size, transcendentals=0),
        name="pick_blocks",
    )(index, source)


def statistics(values):
    centre = jnp.mean(values, axis=1, keepdims=True)
    spread = jnp.mean((values - centre) ** 2, axis=1, keepdims=True)
    inverse_std = lax.rsqrt(spread + EPSILON)
    return (values - centre) * inverse_std, inverse_std


def norm_kernel(index_ref, rows_ref, gain_ref, out_ref):
    normed, _ = statistics(rows_ref[0].astype(F32))
    out_ref[0] = (normed * gain_ref[...]).astype(BF16)


def norm_blocks(index, blocks, gain):
    count, rows, width = blocks.shape
    return pl.pallas_call(
        norm_kernel,
        grid_spec=pltpu.PrefetchScalarGridSpec(
            num_scalar_prefetch=1,
            grid=(count,),
            in_specs=[
                pl.BlockSpec((1, rows, width), lambda i, index: (index[i], 0, 0)),
                pl.BlockSpec((1, width), lambda i, index: (0, 0)),
            ],
            out_specs=pl.BlockSpec((1, rows, width), lambda i, index: (i, 0, 0)),
        ),
        out_shape=jax.ShapeDtypeStruct(blocks.shape, BF16),
        name="norm_blocks",
    )(index, blocks, gain[None])


def norm_back_kernel(index_ref, grads_ref, rows_ref, gain_ref, out_ref):
    normed, inverse_std = statistics(rows_ref[0].astype(F32))
    pushed = grads_ref[0].astype(F32) * gain_ref[...]
    along = jnp.mean(pushed * normed, axis=1, keepdims=True)
    out_ref[0] = (
        inverse_std * (pushed - jnp.mean(pushed, axis=1, keepdims=True) - normed * along)
    ).astype(BF16)


def norm_back(index, grads, blocks, gain):
    count, rows, width = blocks.shape
    return pl.pallas_call(
        norm_back_kernel,
        grid_spec=pltpu.PrefetchScalarGridSpec(
            num_scalar_prefetch=1,
            grid=(count,),
            in_specs=[
                pl.BlockSpec((1, rows, width), lambda i, index: (index[i], 0, 0)),
                pl.BlockSpec((1, rows, width), lambda i, index: (i, 0, 0)),
                pl.BlockSpec((1, width), lambda i, index: (0, 0)),
            ],
            out_specs=pl.BlockSpec((1, rows, width), lambda i, index: (i, 0, 0)),
        ),
        out_shape=jax.ShapeDtypeStruct(blocks.shape, BF16),
        name="norm_back",
    )(index, grads, blocks, gain[None])


GROUPS = 2


def local(loader_rows, lengths, block_order, norm_gain, qkv_weight, upstream_grad):
    seq_count = lax.axis_size(SEQ)
    pack_count = lax.axis_size(DP)
    my_index = lax.axis_index(SEQ)
    _, row_count, model_width = loader_rows.shape
    per_device = row_count // BLK
    order_row = block_order[0]
    block_total = order_row.shape[0]
    piece = BLK * per_device // seq_count
    first, cross, last, back_first, back_cross, back_last = route(my_index, order_row)

    def exchange(x):
        x = x.reshape(seq_count, piece, model_width)
        return lax.all_to_all(x, SEQ, split_axis=0, concat_axis=0, tiled=True)

    up = [(i, i + 1) for i in range(seq_count - 1)]
    down = [(i + 1, i) for i in range(seq_count - 1)]

    def halo(x):
        before = lax.ppermute(x[row_count - BLK :], SEQ, up)
        after = lax.ppermute(x[:BLK], SEQ, down)
        return jnp.concatenate([before, after], axis=0)

    upstream = upstream_grad[0]
    upstream_own = upstream.T
    upstream_halo = halo(upstream).T

    loader_blocks = loader_rows[0].reshape(per_device, BLK, model_width)
    outgoing = norm_blocks(first, loader_blocks, norm_gain)
    spread = exchange(pick(cross, exchange(outgoing)))
    scaled = pick(last, spread.reshape(per_device, BLK, model_width)).reshape(row_count, model_width)
    scaled_halo = halo(scaled)

    def project(rows):
        return lax.dot_general(
            qkv_weight, rows, (((0,), (1,)), ((), ())), preferred_element_type=F32
        ).astype(BF16)

    qkv_own = project(scaled)
    qkv_halo = project(scaled_halo)
    image_ends = jnp.cumsum(lengths[0])
    positions = my_index * row_count - BLK + jnp.arange(row_count + 2 * BLK, dtype=jnp.int32)
    counted = jnp.sum((image_ends[None, :] <= positions[:, None]).astype(jnp.int32), axis=1)
    inside = (positions >= 0) & (positions < block_total * BLK)
    ids = jnp.where(inside, counted, -1)

    pairs = HEADS // 2 // GROUPS
    attended, grads, shares = [], [], []
    for group in range(GROUPS):
        out, grad = attention_call(
            ids, qkv_own, qkv_halo, upstream_own, upstream_halo, group * pairs, pairs
        )
        weight_local = nn(grad, scaled).astype(BF16)
        shares.append(lax.psum_scatter(weight_local, DP, scatter_dimension=0, tiled=True))
        attended.append(out)
        grads.append(grad)
    attention = jnp.concatenate(attended, axis=0).T[None]
    grad_cols = jnp.concatenate(grads, axis=0).reshape(HEADS, 3, HD, row_count)
    grad_cols = grad_cols.transpose(1, 0, 2, 3).reshape(3 * model_width, row_count)
    input_grad = lax.dot_general(
        grad_cols, qkv_weight, (((0,), (1,)), ((), ())), preferred_element_type=F32
    ).astype(BF16)
    returning = pick(back_first, input_grad.reshape(per_device, BLK, model_width))
    returned = exchange(pick(back_cross, exchange(returning)))
    loader_grad = norm_back(
        back_last, returned.reshape(per_device, BLK, model_width), loader_blocks, norm_gain
    ).reshape(1, row_count, model_width)

    share = model_width // seq_count
    per_pack = 3 * model_width // pack_count
    partial = jnp.concatenate(shares, axis=0).T.reshape(seq_count, share, per_pack)
    partial = lax.all_to_all(partial, SEQ, split_axis=0, concat_axis=0, tiled=True)
    summed = jnp.sum(partial.astype(F32), axis=0).astype(BF16)
    weight_cols = lax.all_gather(summed, DP, axis=0)
    heads = HEADS // GROUPS // pack_count
    weight_cols = weight_cols.reshape(pack_count, share, GROUPS, heads, 3, HD)
    weight_grad = weight_cols.transpose(1, 4, 2, 0, 3, 5).reshape(share, 3 * model_width)
    weight_grad = weight_grad.astype(F32) / pack_count
    weight_rows = lax.dynamic_slice_in_dim(qkv_weight, my_index * share, share, 0).astype(F32)
    gain_rows = lax.dynamic_slice_in_dim(norm_gain, my_index * share, share, 0)
    gain_grad = jnp.sum(weight_rows * weight_grad, axis=1) / gain_rows
    return (attention, loader_grad, weight_grad, gain_grad)


def solution(mesh):
    fine = Mesh(mesh.devices.reshape(4, 2, 4, 4), DP + SEQ)
    rows = P(DP, SEQ, None)
    return jax.shard_map(
        local,
        mesh=fine,
        in_specs=(rows, P(DP, None), P(DP, None), P(), P(), rows),
        out_specs=(rows, rows, P(SEQ, None), P(SEQ)),
        check_vma=False,
    )
```

```python
import functools

import jax
import jax.numpy as jnp
from jax import lax
from jax.experimental import pallas as pl
from jax.experimental.pallas import tpu as pltpu
from jax.sharding import Mesh
from jax.sharding import PartitionSpec as P

HEADS = 16
HD = 72
BLK = 128
PAIR = 2 * HD
BF16 = jnp.bfloat16
F32 = jnp.float32
EPSILON = 1e-06
SCORE_SCALE = HD ** (-0.5)
HIDDEN_BIAS = -1e30
DP = ("y", "core")
SEQ = ("z", "x")


def nn(a, b):
    return lax.dot_general(a, b, (((1,), (0,)), ((), ())), preferred_element_type=F32)


def nt(a, b):
    return lax.dot_general(a, b, (((1,), (1,)), ((), ())), preferred_element_type=F32)


def attention_kernel(
    col_ref, row_ref, q_ref, k_ref, v_ref, qh_ref, kh_ref, vh_ref, g_ref, gh_ref,
    o_ref, d_ref, bias_ref, o_s, d_s,
):
    blocks = q_ref.shape[1] // BLK
    rows = q_ref.shape[1]

    @pl.when(pl.program_id(0) == 0)
    def _():
        for b in range(blocks + 2):
            first, last = max(b - 1, 0), min(b + 1, blocks + 1)
            same = col_ref[b * BLK : (b + 1) * BLK, :] == row_ref[:, first * BLK : (last + 1) * BLK]
            bias_ref[b, :, : (last + 1 - first) * BLK] = jnp.where(same, 0.0, HIDDEN_BIAS)

    for head in range(2):
        lo, hi = head * HD, (head + 1) * HD

        def whole(own, halo):
            mid, rim = own[...].astype(F32)[lo:hi], halo[...].astype(F32)[lo:hi]
            return jnp.concatenate([rim[:, :BLK], mid, rim[:, BLK:]], axis=1)

        q32, g32 = whole(q_ref, qh_ref), whole(g_ref, gh_ref)
        q, g = q32.astype(BF16), g32.astype(BF16)
        k, v = whole(k_ref, kh_ref).astype(BF16), whole(v_ref, vh_ref).astype(BF16)
        q_at, k_at, v_at = (slice((3 * head + part) * HD, (3 * head + part + 1) * HD) for part in range(3))
        d_s[k_at, :] = jnp.zeros((HD, rows), F32)
        d_s[v_at, :] = jnp.zeros((HD, rows), F32)
        for b in range(blocks + 2):
            first, last = max(b - 1, 0), min(b + 1, blocks + 1)
            width = (last + 1 - first) * BLK
            k_win = k[:, first * BLK : (last + 1) * BLK]
            v_win = v[:, first * BLK : (last + 1) * BLK]
            here = slice(b * BLK, (b + 1) * BLK)
            scores = nn(q32[:, here].T.astype(BF16), k_win)
            grad_probs = nn(g32[:, here].T.astype(BF16), v_win)
            weights = jnp.exp(scores * SCORE_SCALE + bias_ref[b, :, :width])
            probs = weights * (1.0 / jnp.sum(weights, axis=1, keepdims=True))
            rounded = probs.astype(BF16)
            centred = jnp.sum(probs * grad_probs, axis=1, keepdims=True)
            grad_scores = (probs * (grad_probs - centred) * SCORE_SCALE).astype(BF16)
            if 1 <= b <= blocks:
                own = slice((b - 1) * BLK, b * BLK)
                o_s[lo:hi, own] = nt(v_win, rounded)
                d_s[q_at, own] = nt(k_win, grad_scores)
            k0, k1 = max(first, 1), min(last, blocks)
            seen = slice((k0 - first) * BLK, (k1 + 1 - first) * BLK)
            into = slice((k0 - 1) * BLK, k1 * BLK)
            d_s[k_at, into] += nn(q[:, here], grad_scores[:, seen])
            d_s[v_at, into] += nn(g[:, here], rounded[:, seen])
    o_ref[...] = o_s[...].astype(BF16)
    d_ref[...] = d_s[...].astype(BF16)


def attention_call(ids, own, halo, g_own, g_halo, first_pair, inner):
    rows, rim = own.shape[1], halo.shape[1]
    total, blocks = rows + rim, rows // BLK
    per_part = HEADS // 2
    pairs = 2 * inner

    def spec(width, part):
        return pl.BlockSpec(
            (PAIR, width),
            lambda i: (part * per_part + first_pair + i // inner * (per_part // 2) + i % inner, 0),
        )

    return pl.pallas_call(
        attention_kernel,
        grid=(pairs,),
        in_specs=[
            pl.BlockSpec((total, 1), lambda i: (0, 0)),
            pl.BlockSpec((1, total), lambda i: (0, 0)),
            spec(rows, 0), spec(rows, 1), spec(rows, 2),
            spec(rim, 0), spec(rim, 1), spec(rim, 2),
            spec(rows, 0), spec(rim, 0),
        ],
        out_specs=[
            pl.BlockSpec((PAIR, rows), lambda i: (i, 0)),
            pl.BlockSpec((3 * PAIR, rows), lambda i: (i, 0)),
        ],
        out_shape=[
            jax.ShapeDtypeStruct((pairs * PAIR, rows), BF16),
            jax.ShapeDtypeStruct((pairs * 3 * PAIR, rows), BF16),
        ],
        scratch_shapes=[
            pltpu.VMEM((blocks + 2, BLK, 3 * BLK), F32),
            pltpu.VMEM((PAIR, rows), F32),
            pltpu.VMEM((3 * PAIR, rows), F32),
        ],
        cost_estimate=pl.CostEstimate(
            flops=pairs * 2 * 16 * 12 * BLK * BLK * HD,
            bytes_accessed=pairs * PAIR * (rows * 8 + rim * 4) * 2,
            transcendentals=pairs * 2 * 16 * BLK * BLK,
        ),
        name="packed_attention",
    )(ids[:, None], ids[None, :], own, own, own, halo, halo, halo, g_own, g_halo)


def route_kernel(me_ref, order_ref, first_ref, cross_ref, last_ref, back_first_ref, back_cross_ref, back_last_ref, place, half, hue):
    me = me_ref[0]
    count = order_ref.shape[0]

    def clear(p, _):
        place[order_ref[p]] = p
        half[p] = -1
        hue[p] = -1
        return 0

    lax.fori_loop(0, count, clear, 0)

    def split(bits, partner, mate, seed):
        def start(i, _):
            def step(state):
                at, _ = state
                other = partner(at)
                bits[at] = 0
                bits[other] = 1
                following = mate(other)
                return following, bits[following] < 0

            at = seed(i)
            lax.while_loop(lambda state: state[1], step, (at, bits[at] < 0))
            return 0

        lax.fori_loop(0, count // 2, start, 0)

    split(half, lambda p: p ^ 1, lambda p: place[order_ref[p] ^ 1], lambda i: 2 * i)

    def same_half(p):
        return jnp.where(half[p ^ 2] == half[p], p ^ 2, p ^ 3)

    def same_half_loader(p):
        block = order_ref[p]
        near, far = place[block ^ 2], place[block ^ 3]
        return jnp.where(half[near] == half[p], near, far)

    split(hue, same_half, same_half_loader, lambda i: 4 * (i // 2) + i % 2)

    for slot in range(4):
        at = place[4 * me + slot]
        colour = 2 * half[at] + hue[at]
        first_ref[colour] = slot
        back_last_ref[slot] = colour
        at = 4 * me + slot
        colour = 2 * half[at] + hue[at]
        back_first_ref[colour] = slot
        last_ref[slot] = colour

    mine = me // 4

    def cross(p, _):
        @pl.when(2 * half[p] + hue[p] == mine)
        def _():
            source = order_ref[p] // 4
            cross_ref[p // 4] = source
            back_cross_ref[source] = p // 4

        return 0

    lax.fori_loop(0, count, cross, 0)


def route(me, order):
    smem = pl.BlockSpec(memory_space=pltpu.SMEM)
    sizes = (4, 16, 4, 4, 16, 4)
    return pl.pallas_call(
        route_kernel,
        in_specs=[smem, smem],
        out_specs=[smem] * len(sizes),
        out_shape=[jax.ShapeDtypeStruct((n,), jnp.int32) for n in sizes],
        scratch_shapes=[pltpu.SMEM(order.shape, jnp.int32)] * 3,
        name="route_blocks",
    )(me[None], order)


def pick_kernel(index_ref, source_ref, out_ref):
    for i in range(out_ref.shape[0]):
        out_ref[i] = source_ref[index_ref[i]]


def pick(index, source):
    shape = (index.shape[0],) + source.shape[1:]
    size = 2 * shape[0] * shape[1] * shape[2]
    return pl.pallas_call(
        pick_kernel,
        in_specs=[pl.BlockSpec(memory_space=pltpu.SMEM), pl.BlockSpec(memory_space=pltpu.VMEM)],
        out_specs=pl.BlockSpec(memory_space=pltpu.VMEM),
        out_shape=jax.ShapeDtypeStruct(shape, source.dtype),
        cost_estimate=pl.CostEstimate(flops=0, bytes_accessed=2 * size, transcendentals=0),
        name="pick_blocks",
    )(index, source)


def statistics(values):
    centre = jnp.mean(values, axis=1, keepdims=True)
    spread = jnp.mean((values - centre) ** 2, axis=1, keepdims=True)
    inverse_std = lax.rsqrt(spread + EPSILON)
    return (values - centre) * inverse_std, inverse_std


def norm_kernel(index_ref, rows_ref, gain_ref, out_ref):
    normed, _ = statistics(rows_ref[0].astype(F32))
    out_ref[0] = (normed * gain_ref[...]).astype(BF16)


def norm_blocks(index, blocks, gain):
    count, rows, width = blocks.shape
    return pl.pallas_call(
        norm_kernel,
        grid_spec=pltpu.PrefetchScalarGridSpec(
            num_scalar_prefetch=1,
            grid=(count,),
            in_specs=[
                pl.BlockSpec((1, rows, width), lambda i, index: (index[i], 0, 0)),
                pl.BlockSpec((1, width), lambda i, index: (0, 0)),
            ],
            out_specs=pl.BlockSpec((1, rows, width), lambda i, index: (i, 0, 0)),
        ),
        out_shape=jax.ShapeDtypeStruct(blocks.shape, BF16),
        name="norm_blocks",
    )(index, blocks, gain[None])


def norm_back_kernel(index_ref, grads_ref, rows_ref, gain_ref, out_ref):
    normed, inverse_std = statistics(rows_ref[0].astype(F32))
    pushed = grads_ref[0].astype(F32) * gain_ref[...]
    along = jnp.mean(pushed * normed, axis=1, keepdims=True)
    out_ref[0] = (
        inverse_std * (pushed - jnp.mean(pushed, axis=1, keepdims=True) - normed * along)
    ).astype(BF16)


def norm_back(index, grads, blocks, gain):
    count, rows, width = blocks.shape
    return pl.pallas_call(
        norm_back_kernel,
        grid_spec=pltpu.PrefetchScalarGridSpec(
            num_scalar_prefetch=1,
            grid=(count,),
            in_specs=[
                pl.BlockSpec((1, rows, width), lambda i, index: (index[i], 0, 0)),
                pl.BlockSpec((1, rows, width), lambda i, index: (i, 0, 0)),
                pl.BlockSpec((1, width), lambda i, index: (0, 0)),
            ],
            out_specs=pl.BlockSpec((1, rows, width), lambda i, index: (i, 0, 0)),
        ),
        out_shape=jax.ShapeDtypeStruct(blocks.shape, BF16),
        name="norm_back",
    )(index, grads, blocks, gain[None])


def weight_kernel(place_ref, keep_a, keep_b, got_a, got_b, rows_ref, other_ref, out_ref):
    for part, (keep, got) in enumerate(((keep_a, got_a), (keep_b, got_b))):

        @pl.when(pl.program_id(0) // 2 == part)
        def _():
            out_ref[0] = (nn(keep[0], rows_ref[...]) + nn(got[...], other_ref[...])).astype(BF16)


def weight_product(place, keep, got, rows, other):
    count, width = rows.shape
    block = 3 * HD
    twice = [2 * (keep[0] is keep[1]), 2 * (got[0] is got[1])]

    def first(i):
        return jnp.minimum(i, 1)

    def second(i, skip):
        return jnp.maximum(i - 2, 0) + skip

    whole = pl.BlockSpec((count, width), lambda i, place: (0, 0))
    return pl.pallas_call(
        weight_kernel,
        grid_spec=pltpu.PrefetchScalarGridSpec(
            num_scalar_prefetch=1,
            grid=(4,),
            in_specs=[
                pl.BlockSpec((1, block, count), lambda i, place: (place[0], first(i), 0)),
                pl.BlockSpec((1, block, count), lambda i, place: (place[0], second(i, twice[0]), 0)),
                pl.BlockSpec((block, count), lambda i, place: (first(i), 0)),
                pl.BlockSpec((block, count), lambda i, place: (second(i, twice[1]), 0)),
                whole,
                whole,
            ],
            out_specs=pl.BlockSpec((1, block, width), lambda i, place: (lax.rem(i + 4 - place[1], 4), 0, 0)),
        ),
        out_shape=jax.ShapeDtypeStruct((4, block, width), BF16),
        cost_estimate=pl.CostEstimate(
            flops=16 * block * count * width, bytes_accessed=8 * (block + count) * width, transcendentals=0
        ),
        name="weight_product",
    )(place, *keep, *got, rows, other)


def local(loader_rows, lengths, block_order, norm_gain, qkv_weight, upstream_grad):
    seq_count = lax.axis_size(SEQ)
    pack_count = lax.axis_size(DP)
    my_index = lax.axis_index(SEQ)
    _, row_count, model_width = loader_rows.shape
    per_device = row_count // BLK
    order_row = block_order[0]
    block_total = order_row.shape[0]
    piece = BLK * per_device // seq_count
    first, cross, last, back_first, back_cross, back_last = route(my_index, order_row)

    def exchange(x):
        x = x.reshape(seq_count, piece, model_width)
        return lax.all_to_all(x, SEQ, split_axis=0, concat_axis=0, tiled=True)

    up = [(i, i + 1) for i in range(seq_count - 1)]
    down = [(i + 1, i) for i in range(seq_count - 1)]

    def halo(x):
        before = lax.ppermute(x[row_count - BLK :], SEQ, up)
        after = lax.ppermute(x[:BLK], SEQ, down)
        return jnp.concatenate([before, after], axis=0)

    upstream = upstream_grad[0]
    upstream_own = upstream.T
    upstream_halo = halo(upstream).T

    loader_blocks = loader_rows[0].reshape(per_device, BLK, model_width)
    outgoing = norm_blocks(first, loader_blocks, norm_gain)
    spread = exchange(pick(cross, exchange(outgoing)))
    scaled = pick(last, spread.reshape(per_device, BLK, model_width)).reshape(row_count, model_width)
    scaled_halo = halo(scaled)

    def project(rows):
        return lax.dot_general(
            qkv_weight, rows, (((0,), (1,)), ((), ())), preferred_element_type=F32
        ).astype(BF16)

    qkv_own = project(scaled)
    qkv_halo = project(scaled_halo)
    image_ends = jnp.cumsum(lengths[0])
    positions = my_index * row_count - BLK + jnp.arange(row_count + 2 * BLK, dtype=jnp.int32)
    counted = jnp.sum((image_ends[None, :] <= positions[:, None]).astype(jnp.int32), axis=1)
    inside = (positions >= 0) & (positions < block_total * BLK)
    ids = jnp.where(inside, counted, -1)

    core = lax.axis_index("core")
    place = jnp.stack([core, lax.axis_index("y")])
    swap = [(0, 1), (1, 0)]
    scaled_other = lax.ppermute(scaled, "core", swap)

    def attend(ids, first_pair, inner):
        out, grad = attention_call(
            ids, qkv_own, qkv_halo, upstream_own, upstream_halo, first_pair, inner
        )
        return out.reshape(2, inner * PAIR, row_count), grad.reshape(2, inner * 3 * PAIR, row_count)

    def to_other(grad):
        return lax.ppermute(lax.dynamic_index_in_dim(grad, 1 - core, 0, False), "core", swap)

    along = [(i, (i + 1) % 4) for i in range(4)]
    against = [(j, i) for i, j in along]
    cut = 112

    def over_packs(product):
        own, near, far, last = (product[k] for k in range(4))
        far_up = lax.ppermute(far[:cut], "y", along)
        far_down = lax.ppermute(far[cut:], "y", against)
        near = jnp.concatenate(
            [(near[:cut].astype(F32) + far_up.astype(F32)).astype(BF16), near[cut:]], axis=0
        )
        last = jnp.concatenate(
            [last[:cut], (last[cut:].astype(F32) + far_down.astype(F32)).astype(BF16)], axis=0
        )
        up, down = lax.ppermute(near, "y", along), lax.ppermute(last, "y", against)
        return (own.astype(F32) + up.astype(F32) + down.astype(F32)).astype(BF16)

    share = model_width // seq_count

    def over_rows(part):
        parts = part.T.reshape(seq_count, share, part.shape[0])
        parts = lax.all_to_all(parts, SEQ, split_axis=0, concat_axis=0, tiled=True)
        return jnp.sum(parts.astype(F32), axis=0).astype(BF16)

    out_a, grad_a = attend(ids, 0, 2)
    got_a = to_other(grad_a)
    out_b, grad_b = attend(ids, 2, 1)
    product_a = weight_product(place, (grad_a, grad_a), (got_a, got_a), scaled, scaled_other)
    ids, product_a = lax.optimization_barrier((ids, product_a))
    sum_a = over_packs(product_a)
    got_b = to_other(grad_b)
    out_c, grad_c = attend(ids, 3, 1)
    got_c = to_other(grad_c)
    product_b = weight_product(place, (grad_b, grad_c), (got_b, got_c), scaled, scaled_other)

    sum_b = over_packs(product_b)

    attention = jnp.concatenate([out_a, out_b, out_c], axis=1)
    attention = attention.reshape(model_width, row_count).T[None]
    grad_cols = jnp.concatenate([grad_a, grad_b, grad_c], axis=1).reshape(HEADS, 3, HD, row_count)
    grad_cols = grad_cols.transpose(1, 0, 2, 3).reshape(3 * model_width, row_count)
    grad_cols, product_b = lax.optimization_barrier((grad_cols, product_b))
    input_grad = lax.dot_general(
        grad_cols, qkv_weight, (((0,), (1,)), ((), ())), preferred_element_type=F32
    ).astype(BF16)
    returning = pick(back_first, input_grad.reshape(per_device, BLK, model_width))
    returned = exchange(pick(back_cross, exchange(returning)))
    loader_grad = norm_back(
        back_last, returned.reshape(per_device, BLK, model_width), loader_blocks, norm_gain
    ).reshape(1, row_count, model_width)

    summed = over_rows(jnp.concatenate([sum_a, sum_b], axis=0))
    weight_cols = lax.all_gather(summed, DP, axis=0)
    weight_cols = weight_cols.reshape(4, 2, share, 2, 3, HD)
    weight_grad = weight_cols.transpose(2, 4, 1, 3, 0, 5).reshape(share, 3 * model_width)
    weight_grad = weight_grad.astype(F32) / pack_count
    weight_rows = lax.dynamic_slice_in_dim(qkv_weight, my_index * share, share, 0).astype(F32)
    gain_rows = lax.dynamic_slice_in_dim(norm_gain, my_index * share, share, 0)
    gain_grad = jnp.sum(weight_rows * weight_grad, axis=1) / gain_rows
    return (attention, loader_grad, weight_grad, gain_grad)


def solution(mesh):
    fine = Mesh(mesh.devices.reshape(4, 2, 4, 4), DP + SEQ)
    rows = P(DP, SEQ, None)
    return jax.shard_map(
        local,
        mesh=fine,
        in_specs=(rows, P(DP, None), P(DP, None), P(), P(), rows),
        out_specs=(rows, rows, P(SEQ, None), P(SEQ)),
        check_vma=False,
    )
```

```python
import functools

import jax
import jax.numpy as jnp
from jax import lax
from jax.experimental import pallas as pl
from jax.experimental.pallas import tpu as pltpu
from jax.sharding import Mesh
from jax.sharding import PartitionSpec as P

HEADS = 16
HD = 72
BLK = 128
PAIR = 2 * HD
BF16 = jnp.bfloat16
F32 = jnp.float32
EPSILON = 1e-06
SCORE_SCALE = HD ** (-0.5)
HIDDEN_BIAS = -1e30
DP = ("y", "core")
SEQ = ("z", "x")


def nn(a, b):
    return lax.dot_general(a, b, (((1,), (0,)), ((), ())), preferred_element_type=F32)


def nt(a, b):
    return lax.dot_general(a, b, (((1,), (1,)), ((), ())), preferred_element_type=F32)


def attention_kernel(
    col_ref, row_ref, q_ref, k_ref, v_ref, qh_ref, kh_ref, vh_ref, g_ref, gh_ref,
    o_ref, d_ref, bias_ref, o_s, d_s,
):
    blocks = q_ref.shape[1] // BLK
    rows = q_ref.shape[1]

    @pl.when(pl.program_id(0) == 0)
    def _():
        for b in range(blocks + 2):
            first, last = max(b - 1, 0), min(b + 1, blocks + 1)
            same = col_ref[b * BLK : (b + 1) * BLK, :] == row_ref[:, first * BLK : (last + 1) * BLK]
            bias_ref[b, :, : (last + 1 - first) * BLK] = jnp.where(same, 0.0, HIDDEN_BIAS)

    for head in range(2):
        lo, hi = head * HD, (head + 1) * HD

        def whole(own, halo):
            mid, rim = own[...].astype(F32)[lo:hi], halo[...].astype(F32)[lo:hi]
            return jnp.concatenate([rim[:, :BLK], mid, rim[:, BLK:]], axis=1)

        q32, g32 = whole(q_ref, qh_ref), whole(g_ref, gh_ref)
        q, g = q32.astype(BF16), g32.astype(BF16)
        k, v = whole(k_ref, kh_ref).astype(BF16), whole(v_ref, vh_ref).astype(BF16)
        q_at, k_at, v_at = (slice((3 * head + part) * HD, (3 * head + part + 1) * HD) for part in range(3))
        d_s[k_at, :] = jnp.zeros((HD, rows), F32)
        d_s[v_at, :] = jnp.zeros((HD, rows), F32)
        for b in range(blocks + 2):
            first, last = max(b - 1, 0), min(b + 1, blocks + 1)
            width = (last + 1 - first) * BLK
            k_win = k[:, first * BLK : (last + 1) * BLK]
            v_win = v[:, first * BLK : (last + 1) * BLK]
            here = slice(b * BLK, (b + 1) * BLK)
            scores = nn(q32[:, here].T.astype(BF16), k_win)
            grad_probs = nn(g32[:, here].T.astype(BF16), v_win)
            weights = jnp.exp(scores * SCORE_SCALE + bias_ref[b, :, :width])
            probs = weights * (1.0 / jnp.sum(weights, axis=1, keepdims=True))
            rounded = probs.astype(BF16)
            centred = jnp.sum(probs * grad_probs, axis=1, keepdims=True)
            grad_scores = (probs * (grad_probs - centred) * SCORE_SCALE).astype(BF16)
            if 1 <= b <= blocks:
                own = slice((b - 1) * BLK, b * BLK)
                o_s[lo:hi, own] = nt(v_win, rounded)
                d_s[q_at, own] = nt(k_win, grad_scores)
            k0, k1 = max(first, 1), min(last, blocks)
            seen = slice((k0 - first) * BLK, (k1 + 1 - first) * BLK)
            into = slice((k0 - 1) * BLK, k1 * BLK)
            d_s[k_at, into] += nn(q[:, here], grad_scores[:, seen])
            d_s[v_at, into] += nn(g[:, here], rounded[:, seen])
    o_ref[...] = o_s[...].astype(BF16)
    d_ref[...] = d_s[...].astype(BF16)


def attention_call(ids, own, halo, g_own, g_halo, first_pair=0, pairs=HEADS // 2):
    rows, rim = own.shape[1], halo.shape[1]
    total, blocks = rows + rim, rows // BLK
    per_part = HEADS // 2

    def spec(width, part):
        return pl.BlockSpec((PAIR, width), lambda i: (part * per_part + first_pair + i, 0))

    return pl.pallas_call(
        attention_kernel,
        grid=(pairs,),
        in_specs=[
            pl.BlockSpec((total, 1), lambda i: (0, 0)),
            pl.BlockSpec((1, total), lambda i: (0, 0)),
            spec(rows, 0), spec(rows, 1), spec(rows, 2),
            spec(rim, 0), spec(rim, 1), spec(rim, 2),
            spec(rows, 0), spec(rim, 0),
        ],
        out_specs=[
            pl.BlockSpec((PAIR, rows), lambda i: (i, 0)),
            pl.BlockSpec((3 * PAIR, rows), lambda i: (i, 0)),
        ],
        out_shape=[
            jax.ShapeDtypeStruct((pairs * PAIR, rows), BF16),
            jax.ShapeDtypeStruct((pairs * 3 * PAIR, rows), BF16),
        ],
        scratch_shapes=[
            pltpu.VMEM((blocks + 2, BLK, 3 * BLK), F32),
            pltpu.VMEM((PAIR, rows), F32),
            pltpu.VMEM((3 * PAIR, rows), F32),
        ],
        cost_estimate=pl.CostEstimate(
            flops=pairs * 2 * 16 * 12 * BLK * BLK * HD,
            bytes_accessed=pairs * PAIR * (rows * 8 + rim * 4) * 2,
            transcendentals=pairs * 2 * 16 * BLK * BLK,
        ),
        name="packed_attention",
    )(ids[:, None], ids[None, :], own, own, own, halo, halo, halo, g_own, g_halo)


def route_kernel(me_ref, order_ref, first_ref, cross_ref, last_ref, back_first_ref, back_cross_ref, back_last_ref, place, half, hue):
    me = me_ref[0]
    count = order_ref.shape[0]

    def clear(p, _):
        place[order_ref[p]] = p
        half[p] = -1
        hue[p] = -1
        return 0

    lax.fori_loop(0, count, clear, 0, unroll=8)

    def split(bits, partner, mate, seed):
        def start(i, _):
            def step(state):
                at, _ = state
                other = partner(at)
                bits[at] = 0
                bits[other] = 1
                following = mate(other)
                return following, bits[following] < 0

            at = seed(i)
            lax.while_loop(lambda state: state[1], step, (at, bits[at] < 0))
            return 0

        lax.fori_loop(0, count // 2, start, 0)

    split(half, lambda p: p ^ 1, lambda p: place[order_ref[p] ^ 1], lambda i: 2 * i)

    def same_half(p):
        return jnp.where(half[p ^ 2] == half[p], p ^ 2, p ^ 3)

    def same_half_loader(p):
        block = order_ref[p]
        near, far = place[block ^ 2], place[block ^ 3]
        return jnp.where(half[near] == half[p], near, far)

    split(hue, same_half, same_half_loader, lambda i: 4 * (i // 2) + i % 2)

    for slot in range(4):
        at = place[4 * me + slot]
        colour = 2 * half[at] + hue[at]
        first_ref[colour] = slot
        back_last_ref[slot] = colour
        at = 4 * me + slot
        colour = 2 * half[at] + hue[at]
        back_first_ref[colour] = slot
        last_ref[slot] = colour

    mine = me // 4

    def cross(p, _):
        @pl.when(2 * half[p] + hue[p] == mine)
        def _():
            source = order_ref[p] // 4
            cross_ref[p // 4] = source
            back_cross_ref[source] = p // 4

        return 0

    lax.fori_loop(0, count, cross, 0, unroll=8)


def route(me, order):
    smem = pl.BlockSpec(memory_space=pltpu.SMEM)
    sizes = (4, 16, 4, 4, 16, 4)
    return pl.pallas_call(
        route_kernel,
        in_specs=[smem, smem],
        out_specs=[smem] * len(sizes),
        out_shape=[jax.ShapeDtypeStruct((n,), jnp.int32) for n in sizes],
        scratch_shapes=[pltpu.SMEM(order.shape, jnp.int32)] * 3,
        name="route_blocks",
    )(me[None], order)


def pick_kernel(index_ref, source_ref, out_ref):
    for i in range(out_ref.shape[0]):
        out_ref[i] = source_ref[index_ref[i]]


def pick(index, source):
    return whole_call(pick_kernel, index, source, name="pick_blocks")


def statistics(values):
    centre = jnp.mean(values, axis=1, keepdims=True)
    spread = jnp.mean((values - centre) ** 2, axis=1, keepdims=True)
    inverse_std = lax.rsqrt(spread + EPSILON)
    return (values - centre) * inverse_std, inverse_std


def norm_kernel(index_ref, rows_ref, gain_ref, out_ref):
    for i in range(out_ref.shape[0]):
        normed, _ = statistics(rows_ref[index_ref[i]].astype(F32))
        out_ref[i] = (normed * gain_ref[...][None]).astype(BF16)


def whole_call(kernel, index, *arrays, name):
    size = 2 * (1 + len(arrays)) * arrays[0].size
    return pl.pallas_call(
        kernel,
        in_specs=[pl.BlockSpec(memory_space=pltpu.SMEM)]
        + [pl.BlockSpec(memory_space=pltpu.VMEM)] * len(arrays),
        out_specs=pl.BlockSpec(memory_space=pltpu.VMEM),
        out_shape=jax.ShapeDtypeStruct((index.shape[0],) + arrays[0].shape[1:], BF16),
        compiler_params=pltpu.CompilerParams(vmem_limit_bytes=16 * 2**20),
        cost_estimate=pl.CostEstimate(flops=size, bytes_accessed=size, transcendentals=0),
        name=name,
    )(index, *arrays)


def norm_blocks(index, blocks, gain):
    return whole_call(norm_kernel, index, blocks, gain, name="norm_blocks")


def norm_back_kernel(index_ref, grads_ref, rows_ref, gain_ref, out_ref):
    for i in range(out_ref.shape[0]):
        normed, inverse_std = statistics(rows_ref[i].astype(F32))
        pushed = grads_ref[index_ref[i]].astype(F32) * gain_ref[...][None]
        along = jnp.mean(pushed * normed, axis=1, keepdims=True)
        out_ref[i] = (
            inverse_std * (pushed - jnp.mean(pushed, axis=1, keepdims=True) - normed * along)
        ).astype(BF16)


def norm_back(index, grads, blocks, gain):
    return whole_call(norm_back_kernel, index, grads, blocks, gain, name="norm_back")


GROUPS = 1


def local(loader_rows, lengths, block_order, norm_gain, qkv_weight, upstream_grad):
    seq_count = lax.axis_size(SEQ)
    pack_count = lax.axis_size(DP)
    my_index = lax.axis_index(SEQ)
    _, row_count, model_width = loader_rows.shape
    per_device = row_count // BLK
    order_row = block_order[0]
    block_total = order_row.shape[0]
    piece = BLK * per_device // seq_count
    first, cross, last, back_first, back_cross, back_last = route(my_index, order_row)

    def exchange(x):
        x = x.reshape(seq_count, piece, model_width)
        return lax.all_to_all(x, SEQ, split_axis=0, concat_axis=0, tiled=True)

    up = [(i, i + 1) for i in range(seq_count - 1)]
    down = [(i + 1, i) for i in range(seq_count - 1)]

    def halo(x):
        before = lax.ppermute(x[row_count - BLK :], SEQ, up)
        after = lax.ppermute(x[:BLK], SEQ, down)
        return jnp.concatenate([before, after], axis=0)

    upstream = upstream_grad[0]
    upstream_own = upstream.T
    upstream_halo = halo(upstream).T

    loader_blocks = loader_rows[0].reshape(per_device, BLK, model_width)
    outgoing = norm_blocks(first, loader_blocks, norm_gain)
    spread = exchange(pick(cross, exchange(outgoing)))
    scaled = pick(last, spread.reshape(per_device, BLK, model_width)).reshape(row_count, model_width)
    scaled_halo = halo(scaled)

    def project(rows):
        return lax.dot_general(
            qkv_weight, rows, (((0,), (1,)), ((), ())), preferred_element_type=F32
        ).astype(BF16)

    qkv_own = project(scaled)
    qkv_halo = project(scaled_halo)
    image_ends = jnp.cumsum(lengths[0])
    positions = my_index * row_count - BLK + jnp.arange(row_count + 2 * BLK, dtype=jnp.int32)
    counted = jnp.sum((image_ends[None, :] <= positions[:, None]).astype(jnp.int32), axis=1)
    inside = (positions >= 0) & (positions < block_total * BLK)
    ids = jnp.where(inside, counted, -1)

    pairs = HEADS // 2 // GROUPS
    attended, grads, shares = [], [], []
    for group in range(GROUPS):
        out, grad = attention_call(
            ids, qkv_own, qkv_halo, upstream_own, upstream_halo, group * pairs, pairs
        )
        weight_local = nn(grad, scaled).astype(BF16)
        shares.append(lax.psum_scatter(weight_local, DP, scatter_dimension=0, tiled=True))
        attended.append(out)
        grads.append(grad)
    attention = jnp.concatenate(attended, axis=0).T[None]
    grad_cols = jnp.concatenate(grads, axis=0).reshape(HEADS, 3, HD, row_count)
    grad_cols = grad_cols.transpose(1, 0, 2, 3).reshape(3 * model_width, row_count)
    input_grad = lax.dot_general(
        grad_cols, qkv_weight, (((0,), (1,)), ((), ())), preferred_element_type=F32
    ).astype(BF16)
    returning = pick(back_first, input_grad.reshape(per_device, BLK, model_width))
    returned = exchange(pick(back_cross, exchange(returning)))
    loader_grad = norm_back(
        back_last, returned.reshape(per_device, BLK, model_width), loader_blocks, norm_gain
    ).reshape(1, row_count, model_width)

    share = model_width // seq_count
    per_pack = 3 * model_width // pack_count
    partial = jnp.concatenate(shares, axis=0).T.reshape(seq_count, share, per_pack)
    partial = lax.all_to_all(partial, SEQ, split_axis=0, concat_axis=0, tiled=True)
    summed = jnp.sum(partial.astype(F32), axis=0).astype(BF16)
    weight_cols = lax.all_gather(summed, DP, axis=0)
    heads = HEADS // GROUPS // pack_count
    weight_cols = weight_cols.reshape(pack_count, share, GROUPS, heads, 3, HD)
    weight_grad = weight_cols.transpose(1, 4, 2, 0, 3, 5).reshape(share, 3 * model_width)
    weight_grad = weight_grad.astype(F32) / pack_count
    weight_rows = lax.dynamic_slice_in_dim(qkv_weight, my_index * share, share, 0).astype(F32)
    gain_rows = lax.dynamic_slice_in_dim(norm_gain, my_index * share, share, 0)
    gain_grad = jnp.sum(weight_rows * weight_grad, axis=1) / gain_rows
    return (attention, loader_grad, weight_grad, gain_grad)


def solution(mesh):
    fine = Mesh(mesh.devices.reshape(4, 2, 4, 4), DP + SEQ)
    rows = P(DP, SEQ, None)
    return jax.shard_map(
        local,
        mesh=fine,
        in_specs=(rows, P(DP, None), P(DP, None), P(), P(), rows),
        out_specs=(rows, rows, P(SEQ, None), P(SEQ)),
        check_vma=False,
    )
```

```python
import functools

import jax
import jax.numpy as jnp
from jax import lax
from jax.experimental import pallas as pl
from jax.experimental.pallas import tpu as pltpu
from jax.sharding import Mesh
from jax.sharding import PartitionSpec as P

HEADS = 16
HD = 72
BLK = 128
PAIR = 2 * HD
BF16 = jnp.bfloat16
F32 = jnp.float32
EPSILON = 1e-06
SCORE_SCALE = HD ** (-0.5)
EXP2_SCALE = SCORE_SCALE * 1.4426950408889634
HIDDEN_BIAS = -1e30
LAG = 2
DP = ("y", "core")
SEQ = ("z", "x")


def nn(a, b):
    return lax.dot_general(a, b, (((1,), (0,)), ((), ())), preferred_element_type=F32)


def nt(a, b):
    return lax.dot_general(a, b, (((1,), (1,)), ((), ())), preferred_element_type=F32)


def attention_kernel(
    col_ref, row_ref, q_ref, k_ref, v_ref, qh_ref, kh_ref, vh_ref, g_ref, gh_ref,
    o_ref, d_ref, bias_ref, o_s, d_s,
):
    blocks = q_ref.shape[1] // BLK
    rows = q_ref.shape[1]

    @pl.when(pl.program_id(0) == 0)
    def _():
        for b in range(blocks + 2):
            first, last = max(b - 1, 0), min(b + 1, blocks + 1)
            same = col_ref[b * BLK : (b + 1) * BLK, :] == row_ref[:, first * BLK : (last + 1) * BLK]
            bias_ref[b, :, : (last + 1 - first) * BLK] = jnp.where(same, 0.0, HIDDEN_BIAS)

    def operands(head):
        lo, hi = head * HD, (head + 1) * HD

        def whole(own, halo):
            mid, rim = own[...].astype(F32)[lo:hi], halo[...].astype(F32)[lo:hi]
            return jnp.concatenate([rim[:, :BLK], mid, rim[:, BLK:]], axis=1)

        q32, g32 = whole(q_ref, qh_ref), whole(g_ref, gh_ref)
        k, v = whole(k_ref, kh_ref).astype(BF16), whole(v_ref, vh_ref).astype(BF16)
        return q32, g32, q32.astype(BF16), g32.astype(BF16), k, v

    heads = [operands(head) for head in range(2)]
    for part in (1, 2, 4, 5):
        d_s[part * HD : (part + 1) * HD, :] = jnp.zeros((HD, rows), F32)

    def window(b):
        first, last = max(b - 1, 0), min(b + 1, blocks + 1)
        return first, last, slice(first * BLK, (last + 1) * BLK), slice(b * BLK, (b + 1) * BLK)

    def products(head, b):
        q32, g32, _, _, k, v = heads[head]
        _, _, near, here = window(b)
        scores = nn(q32[:, here].T.astype(BF16), k[:, near])
        grad_probs = nn(g32[:, here].T.astype(BF16), v[:, near])
        return scores, grad_probs

    def softmax(head, b, scores, grad_probs):
        weights = jnp.exp2(scores * EXP2_SCALE + bias_ref[b, :, : scores.shape[1]])
        probs = weights * (1.0 / jnp.sum(weights, axis=1, keepdims=True))
        centred = jnp.sum(probs * grad_probs, axis=1, keepdims=True)
        return probs.astype(BF16), (probs * (grad_probs - centred)).astype(BF16)

    def results(head, b, rounded, grad_scores):
        _, _, q, g, k, v = heads[head]
        first, last, near, here = window(b)
        q_at, k_at, v_at = (slice((3 * head + part) * HD, (3 * head + part + 1) * HD) for part in range(3))
        if 1 <= b <= blocks:
            own = slice((b - 1) * BLK, b * BLK)
            o_s[head * HD : (head + 1) * HD, own] = nt(v[:, near], rounded)
            d_s[q_at, own] = nt(k[:, near], grad_scores)
        k0, k1 = max(first, 1), min(last, blocks)
        seen = slice((k0 - first) * BLK, (k1 + 1 - first) * BLK)
        into = slice((k0 - 1) * BLK, k1 * BLK)
        d_s[k_at, into] += nn(q[:, here], grad_scores[:, seen])
        d_s[v_at, into] += nn(g[:, here], rounded[:, seen])

    items = [(head, b) for b in range(blocks + 2) for head in range(2)]
    scored, softened = {}, {}
    for step in range(len(items) + 2 * LAG):
        if step < len(items):
            scored[step] = products(*items[step])
        if 0 <= step - LAG < len(items):
            softened[step - LAG] = softmax(*items[step - LAG], *scored.pop(step - LAG))
        if 0 <= step - 2 * LAG:
            results(*items[step - 2 * LAG], *softened.pop(step - 2 * LAG))
    o_ref[...] = o_s[...].astype(BF16)
    for head in range(2):
        for part, factor in enumerate((SCORE_SCALE, SCORE_SCALE, None)):
            at = slice((3 * head + part) * HD, (3 * head + part + 1) * HD)
            if factor is not None:
                d_s[at, :] = d_s[at, :] * factor
    d_ref[...] = d_s[...].astype(BF16)


def attention_call(ids, own, halo, g_own, g_halo, first_pair=0, pairs=HEADS // 2):
    rows, rim = own.shape[1], halo.shape[1]
    total, blocks = rows + rim, rows // BLK
    per_part = HEADS // 2

    def spec(width, part):
        return pl.BlockSpec((PAIR, width), lambda i: (part * per_part + first_pair + i, 0))

    return pl.pallas_call(
        attention_kernel,
        grid=(pairs,),
        in_specs=[
            pl.BlockSpec((total, 1), lambda i: (0, 0)),
            pl.BlockSpec((1, total), lambda i: (0, 0)),
            spec(rows, 0), spec(rows, 1), spec(rows, 2),
            spec(rim, 0), spec(rim, 1), spec(rim, 2),
            spec(rows, 0), spec(rim, 0),
        ],
        out_specs=[
            pl.BlockSpec((PAIR, rows), lambda i: (i, 0)),
            pl.BlockSpec((3 * PAIR, rows), lambda i: (i, 0)),
        ],
        out_shape=[
            jax.ShapeDtypeStruct((pairs * PAIR, rows), BF16),
            jax.ShapeDtypeStruct((pairs * 3 * PAIR, rows), BF16),
        ],
        scratch_shapes=[
            pltpu.VMEM((blocks + 2, BLK, 3 * BLK), F32),
            pltpu.VMEM((PAIR, rows), F32),
            pltpu.VMEM((3 * PAIR, rows), F32),
        ],
        cost_estimate=pl.CostEstimate(
            flops=pairs * 2 * 16 * 12 * BLK * BLK * HD,
            bytes_accessed=pairs * PAIR * (rows * 8 + rim * 4) * 2,
            transcendentals=pairs * 2 * 16 * BLK * BLK,
        ),
        name="packed_attention",
    )(ids[:, None], ids[None, :], own, own, own, halo, halo, halo, g_own, g_halo)


def route_kernel(
    me_ref, order_ref, rows_ref, gain_ref,
    out_ref, first_ref, cross_ref, last_ref, back_first_ref, back_cross_ref, back_last_ref,
    place, half, hue, buffer, arrived,
):
    fetch = pltpu.make_async_copy(rows_ref, buffer, arrived)
    fetch.start()
    me = me_ref[0]
    count = order_ref.shape[0]

    def clear(p, _):
        place[order_ref[p]] = p
        half[p] = -1
        hue[p] = -1
        return 0

    lax.fori_loop(0, count, clear, 0, unroll=8)

    def split(bits, partner, mate, seed):
        def start(i, _):
            def step(state):
                at, _ = state
                other = partner(at)
                bits[at] = 0
                bits[other] = 1
                following = mate(other)
                return following, bits[following] < 0

            at = seed(i)
            lax.while_loop(lambda state: state[1], step, (at, bits[at] < 0))
            return 0

        lax.fori_loop(0, count // 2, start, 0)

    split(half, lambda p: p ^ 1, lambda p: place[order_ref[p] ^ 1], lambda i: 2 * i)

    def same_half(p):
        return jnp.where(half[p ^ 2] == half[p], p ^ 2, p ^ 3)

    def same_half_loader(p):
        block = order_ref[p]
        near, far = place[block ^ 2], place[block ^ 3]
        return jnp.where(half[near] == half[p], near, far)

    split(hue, same_half, same_half_loader, lambda i: 4 * (i // 2) + i % 2)

    for slot in range(4):
        at = place[4 * me + slot]
        colour = 2 * half[at] + hue[at]
        first_ref[colour] = slot
        back_last_ref[slot] = colour
        at = 4 * me + slot
        colour = 2 * half[at] + hue[at]
        back_first_ref[colour] = slot
        last_ref[slot] = colour

    mine = me // 4

    def cross(p, _):
        @pl.when(2 * half[p] + hue[p] == mine)
        def _():
            source = order_ref[p] // 4
            cross_ref[p // 4] = source
            back_cross_ref[source] = p // 4

        return 0

    lax.fori_loop(0, count, cross, 0, unroll=8)
    fetch.wait()
    for i in range(out_ref.shape[0]):
        normed, _ = statistics(buffer[first_ref[i]].astype(F32))
        out_ref[i] = (normed * gain_ref[...][None]).astype(BF16)


def route(me, order, blocks, gain):
    smem = pl.BlockSpec(memory_space=pltpu.SMEM)
    vmem = pl.BlockSpec(memory_space=pltpu.VMEM)
    sizes = (4, 16, 4, 4, 16, 4)
    return pl.pallas_call(
        route_kernel,
        in_specs=[smem, smem, pl.BlockSpec(memory_space=pl.ANY), vmem],
        out_specs=[vmem] + [smem] * len(sizes),
        out_shape=[jax.ShapeDtypeStruct(blocks.shape, BF16)]
        + [jax.ShapeDtypeStruct((n,), jnp.int32) for n in sizes],
        scratch_shapes=[pltpu.SMEM(order.shape, jnp.int32)] * 3
        + [pltpu.VMEM(blocks.shape, BF16), pltpu.SemaphoreType.DMA(())],
        name="route_blocks",
    )(me[None], order, blocks, gain)


def pick_kernel(index_ref, source_ref, out_ref):
    for i in range(out_ref.shape[0]):
        out_ref[i] = source_ref[index_ref[i]]


def pick(index, source):
    return whole_call(pick_kernel, index, source, name="pick_blocks")


def statistics(values):
    centre = jnp.mean(values, axis=1, keepdims=True)
    spread = jnp.mean((values - centre) ** 2, axis=1, keepdims=True)
    inverse_std = lax.rsqrt(spread + EPSILON)
    return (values - centre) * inverse_std, inverse_std


def whole_call(kernel, index, *arrays, name):
    size = 2 * (1 + len(arrays)) * arrays[0].size
    return pl.pallas_call(
        kernel,
        in_specs=[pl.BlockSpec(memory_space=pltpu.SMEM)]
        + [pl.BlockSpec(memory_space=pltpu.VMEM)] * len(arrays),
        out_specs=pl.BlockSpec(memory_space=pltpu.VMEM),
        out_shape=jax.ShapeDtypeStruct((index.shape[0],) + arrays[0].shape[1:], BF16),
        compiler_params=pltpu.CompilerParams(vmem_limit_bytes=16 * 2**20),
        cost_estimate=pl.CostEstimate(flops=size, bytes_accessed=size, transcendentals=0),
        name=name,
    )(index, *arrays)


def norm_back_kernel(index_ref, grads_ref, rows_ref, gain_ref, out_ref):
    for i in range(out_ref.shape[0]):
        normed, inverse_std = statistics(rows_ref[i].astype(F32))
        pushed = grads_ref[index_ref[i]].astype(F32) * gain_ref[...][None]
        along = jnp.mean(pushed * normed, axis=1, keepdims=True)
        out_ref[i] = (
            inverse_std * (pushed - jnp.mean(pushed, axis=1, keepdims=True) - normed * along)
        ).astype(BF16)


def norm_back(index, grads, blocks, gain):
    return whole_call(norm_back_kernel, index, grads, blocks, gain, name="norm_back")


def assemble_kernel(parts_ref, weight_ref, gain_ref, out_ref, gain_grad_ref):
    packs, share, _ = parts_ref.shape
    heads = HEADS // packs
    width = out_ref.shape[1] // 3
    for pack in range(packs):
        cols = parts_ref[pack].astype(F32) * (1.0 / packs)
        for head in range(heads):
            for part in range(3):
                at = part * width + (pack * heads + head) * HD
                start = (3 * head + part) * HD
                out_ref[:, at : at + HD] = cols[:, start : start + HD]
    total = jnp.sum(out_ref[...] * weight_ref[...].astype(F32), axis=1, keepdims=True)
    gain_grad_ref[...] = total / gain_ref[...]


def assemble(parts, weight_rows, gain_rows):
    packs, share, per_pack = parts.shape
    vmem = pl.BlockSpec(memory_space=pltpu.VMEM)
    return pl.pallas_call(
        assemble_kernel,
        in_specs=[vmem] * 3,
        out_specs=[vmem] * 2,
        out_shape=[
            jax.ShapeDtypeStruct((share, packs * per_pack), F32),
            jax.ShapeDtypeStruct((share, 1), F32),
        ],
        compiler_params=pltpu.CompilerParams(vmem_limit_bytes=16 * 2**20),
        name="assemble",
    )(parts, weight_rows, gain_rows)


def local(loader_rows, lengths, block_order, norm_gain, qkv_weight, upstream_grad):
    seq_count = lax.axis_size(SEQ)
    pack_count = lax.axis_size(DP)
    my_index = lax.axis_index(SEQ)
    _, row_count, model_width = loader_rows.shape
    per_device = row_count // BLK
    order_row = block_order[0]
    block_total = order_row.shape[0]
    piece = BLK * per_device // seq_count
    loader_blocks = loader_rows[0].reshape(per_device, BLK, model_width)
    outgoing, _, cross, last, back_first, back_cross, back_last = route(
        my_index, order_row, loader_blocks, norm_gain
    )

    def exchange(x):
        x = x.reshape(seq_count, piece, model_width)
        return lax.all_to_all(x, SEQ, split_axis=0, concat_axis=0, tiled=True)

    up = [(i, i + 1) for i in range(seq_count - 1)]
    down = [(i + 1, i) for i in range(seq_count - 1)]

    def halo(x):
        before = lax.ppermute(x[row_count - BLK :], SEQ, up)
        after = lax.ppermute(x[:BLK], SEQ, down)
        return jnp.concatenate([before, after], axis=0)

    upstream = upstream_grad[0]
    upstream_own = upstream.T
    upstream_halo = halo(upstream).T

    spread = exchange(pick(cross, exchange(outgoing)))
    scaled = pick(last, spread.reshape(per_device, BLK, model_width)).reshape(row_count, model_width)
    scaled_halo = halo(scaled)

    def project(rows):
        return lax.dot_general(
            qkv_weight, rows, (((0,), (1,)), ((), ())), preferred_element_type=F32
        ).astype(BF16)

    qkv_own = project(scaled)
    qkv_halo = project(scaled_halo)
    image_ends = jnp.cumsum(lengths[0])
    positions = my_index * row_count - BLK + jnp.arange(row_count + 2 * BLK, dtype=jnp.int32)
    counted = jnp.sum((image_ends[None, :] <= positions[:, None]).astype(jnp.int32), axis=1)
    inside = (positions >= 0) & (positions < block_total * BLK)
    ids = jnp.where(inside, counted, -1)

    attended, grads = attention_call(ids, qkv_own, qkv_halo, upstream_own, upstream_halo)
    weight_local = nn(grads, scaled).astype(BF16)
    weight_part = lax.psum_scatter(weight_local, DP, scatter_dimension=0, tiled=True)
    attention = attended.T[None]
    grad_cols = grads.reshape(HEADS, 3, HD, row_count)
    grad_cols = grad_cols.transpose(1, 0, 2, 3).reshape(3 * model_width, row_count)
    input_grad = lax.dot_general(
        grad_cols, qkv_weight, (((0,), (1,)), ((), ())), preferred_element_type=F32
    ).astype(BF16)
    returning = pick(back_first, input_grad.reshape(per_device, BLK, model_width))
    returned = exchange(pick(back_cross, exchange(returning)))
    loader_grad = norm_back(
        back_last, returned.reshape(per_device, BLK, model_width), loader_blocks, norm_gain
    ).reshape(1, row_count, model_width)

    share = model_width // seq_count
    per_pack = 3 * model_width // pack_count
    partial = weight_part.T.reshape(seq_count, share, per_pack)
    partial = lax.all_to_all(partial, SEQ, split_axis=0, concat_axis=0, tiled=True)
    summed = jnp.sum(partial.astype(F32), axis=0).astype(BF16)
    weight_cols = lax.all_gather(summed, DP, axis=0)
    weight_rows = lax.dynamic_slice_in_dim(qkv_weight, my_index * share, share, 0)
    gain_rows = lax.dynamic_slice_in_dim(norm_gain, my_index * share, share, 0)[:, None]
    weight_grad, gain_grad = assemble(weight_cols, weight_rows, gain_rows)
    gain_grad = gain_grad[:, 0]
    return (attention, loader_grad, weight_grad, gain_grad)


def solution(mesh):
    fine = Mesh(mesh.devices.reshape(4, 2, 4, 4), DP + SEQ)
    rows = P(DP, SEQ, None)
    return jax.shard_map(
        local,
        mesh=fine,
        in_specs=(rows, P(DP, None), P(DP, None), P(), P(), rows),
        out_specs=(rows, rows, P(SEQ, None), P(SEQ)),
        check_vma=False,
    )
```

```python
import functools

import jax
import jax.numpy as jnp
from jax import lax
from jax.experimental import pallas as pl
from jax.experimental.pallas import tpu as pltpu
from jax.sharding import Mesh
from jax.sharding import PartitionSpec as P

HEADS = 16
HD = 72
BLK = 128
PAIR = 2 * HD
BF16 = jnp.bfloat16
F32 = jnp.float32
EPSILON = 1e-06
SCORE_SCALE = HD ** (-0.5)
EXP2_SCALE = SCORE_SCALE * 1.4426950408889634
HIDDEN_BIAS = -1e30
LAG = 2
DP = ("y", "core")
SEQ = ("z", "x")


def nn(a, b):
    return lax.dot_general(a, b, (((1,), (0,)), ((), ())), preferred_element_type=F32)


def nt(a, b):
    return lax.dot_general(a, b, (((1,), (1,)), ((), ())), preferred_element_type=F32)


def attention_kernel(
    col_ref, row_ref, q_ref, k_ref, v_ref, qh_ref, kh_ref, vh_ref, g_ref, gh_ref, rows_ref,
    o_ref, d_ref, w_ref, bias_ref, o_s, d_s,
):
    blocks = q_ref.shape[1] // BLK
    rows = q_ref.shape[1]

    @pl.when(pl.program_id(0) == 0)
    def _():
        for b in range(blocks + 2):
            first, last = max(b - 1, 0), min(b + 1, blocks + 1)
            same = col_ref[b * BLK : (b + 1) * BLK, :] == row_ref[:, first * BLK : (last + 1) * BLK]
            bias_ref[b, :, : (last + 1 - first) * BLK] = jnp.where(same, 0.0, HIDDEN_BIAS)

    def operands(head):
        lo, hi = head * HD, (head + 1) * HD

        def whole(own, halo):
            mid, rim = own[...].astype(F32)[lo:hi], halo[...].astype(F32)[lo:hi]
            return jnp.concatenate([rim[:, :BLK], mid, rim[:, BLK:]], axis=1)

        q32, g32 = whole(q_ref, qh_ref), whole(g_ref, gh_ref)
        k, v = whole(k_ref, kh_ref).astype(BF16), whole(v_ref, vh_ref).astype(BF16)
        return q32, g32, q32.astype(BF16), g32.astype(BF16), k, v

    heads = [operands(head) for head in range(2)]
    for part in (1, 2, 4, 5):
        d_s[part * HD : (part + 1) * HD, :] = jnp.zeros((HD, rows), F32)

    def window(b):
        first, last = max(b - 1, 0), min(b + 1, blocks + 1)
        return first, last, slice(first * BLK, (last + 1) * BLK), slice(b * BLK, (b + 1) * BLK)

    def products(head, b):
        q32, g32, _, _, k, v = heads[head]
        _, _, near, here = window(b)
        scores = nn(q32[:, here].T.astype(BF16), k[:, near])
        grad_probs = nn(g32[:, here].T.astype(BF16), v[:, near])
        return scores, grad_probs

    def softmax(head, b, scores, grad_probs):
        weights = jnp.exp2(scores * EXP2_SCALE + bias_ref[b, :, : scores.shape[1]])
        probs = weights * (1.0 / jnp.sum(weights, axis=1, keepdims=True))
        centred = jnp.sum(probs * grad_probs, axis=1, keepdims=True)
        return probs.astype(BF16), (probs * (grad_probs - centred)).astype(BF16)

    def results(head, b, rounded, grad_scores):
        _, _, q, g, k, v = heads[head]
        first, last, near, here = window(b)
        q_at, k_at, v_at = (slice((3 * head + part) * HD, (3 * head + part + 1) * HD) for part in range(3))
        if 1 <= b <= blocks:
            own = slice((b - 1) * BLK, b * BLK)
            o_s[head * HD : (head + 1) * HD, own] = nt(v[:, near], rounded)
            d_s[q_at, own] = nt(k[:, near], grad_scores)
        k0, k1 = max(first, 1), min(last, blocks)
        seen = slice((k0 - first) * BLK, (k1 + 1 - first) * BLK)
        into = slice((k0 - 1) * BLK, k1 * BLK)
        d_s[k_at, into] += nn(q[:, here], grad_scores[:, seen])
        d_s[v_at, into] += nn(g[:, here], rounded[:, seen])

    items = [(head, b) for b in range(blocks + 2) for head in range(2)]
    scored, softened = {}, {}
    for step in range(len(items) + 2 * LAG):
        if step < len(items):
            scored[step] = products(*items[step])
        if 0 <= step - LAG < len(items):
            softened[step - LAG] = softmax(*items[step - LAG], *scored.pop(step - LAG))
        if 0 <= step - 2 * LAG:
            results(*items[step - 2 * LAG], *softened.pop(step - 2 * LAG))
    o_ref[...] = o_s[...].astype(BF16)
    for head in range(2):
        for part, factor in enumerate((SCORE_SCALE, SCORE_SCALE, None)):
            at = slice((3 * head + part) * HD, (3 * head + part + 1) * HD)
            if factor is not None:
                d_s[at, :] = d_s[at, :] * factor
    grads = d_s[...].astype(BF16)
    d_ref[...] = grads
    third = rows_ref.shape[1] // 3
    for part in range(3):
        cols = slice(part * third, (part + 1) * third)
        w_ref[:, cols] = nn(grads, rows_ref[:, cols]).astype(BF16)


def attention_call(ids, own, halo, g_own, g_halo, scaled, first_pair=0, pairs=HEADS // 2):
    rows, rim = own.shape[1], halo.shape[1]
    total, blocks = rows + rim, rows // BLK
    per_part = HEADS // 2

    def spec(width, part):
        return pl.BlockSpec((PAIR, width), lambda i: (part * per_part + first_pair + i, 0))

    return pl.pallas_call(
        attention_kernel,
        grid=(pairs,),
        in_specs=[
            pl.BlockSpec((total, 1), lambda i: (0, 0)),
            pl.BlockSpec((1, total), lambda i: (0, 0)),
            spec(rows, 0), spec(rows, 1), spec(rows, 2),
            spec(rim, 0), spec(rim, 1), spec(rim, 2),
            spec(rows, 0), spec(rim, 0),
            pl.BlockSpec(scaled.shape, lambda i: (0, 0)),
        ],
        out_specs=[
            pl.BlockSpec((PAIR, rows), lambda i: (i, 0)),
            pl.BlockSpec((3 * PAIR, rows), lambda i: (i, 0)),
            pl.BlockSpec((3 * PAIR, scaled.shape[1]), lambda i: (i, 0)),
        ],
        out_shape=[
            jax.ShapeDtypeStruct((pairs * PAIR, rows), BF16),
            jax.ShapeDtypeStruct((pairs * 3 * PAIR, rows), BF16),
            jax.ShapeDtypeStruct((pairs * 3 * PAIR, scaled.shape[1]), BF16),
        ],
        scratch_shapes=[
            pltpu.VMEM((blocks + 2, BLK, 3 * BLK), F32),
            pltpu.VMEM((PAIR, rows), F32),
            pltpu.VMEM((3 * PAIR, rows), F32),
        ],
        cost_estimate=pl.CostEstimate(
            flops=pairs * 2 * 16 * 12 * BLK * BLK * HD,
            bytes_accessed=pairs * PAIR * (rows * 8 + rim * 4) * 2,
            transcendentals=pairs * 2 * 16 * BLK * BLK,
        ),
        name="packed_attention",
    )(ids[:, None], ids[None, :], own, own, own, halo, halo, halo, g_own, g_halo, scaled)


def route_kernel(
    me_ref, order_ref, rows_ref, gain_ref,
    out_ref, first_ref, cross_ref, last_ref, back_first_ref, back_cross_ref, back_last_ref,
    place, half, hue, buffer, arrived,
):
    fetch = pltpu.make_async_copy(rows_ref, buffer, arrived)
    fetch.start()
    me = me_ref[0]
    count = order_ref.shape[0]

    def clear(p, _):
        place[order_ref[p]] = p
        half[p] = -1
        hue[p] = -1
        return 0

    lax.fori_loop(0, count, clear, 0, unroll=8)

    def split(bits, partner, mate, seed):
        def start(i, _):
            def step(state):
                at, _ = state
                other = partner(at)
                bits[at] = 0
                bits[other] = 1
                following = mate(other)
                return following, bits[following] < 0

            at = seed(i)
            lax.while_loop(lambda state: state[1], step, (at, bits[at] < 0))
            return 0

        lax.fori_loop(0, count // 2, start, 0)

    split(half, lambda p: p ^ 1, lambda p: place[order_ref[p] ^ 1], lambda i: 2 * i)

    def same_half(p):
        return jnp.where(half[p ^ 2] == half[p], p ^ 2, p ^ 3)

    def same_half_loader(p):
        block = order_ref[p]
        near, far = place[block ^ 2], place[block ^ 3]
        return jnp.where(half[near] == half[p], near, far)

    split(hue, same_half, same_half_loader, lambda i: 4 * (i // 2) + i % 2)

    for slot in range(4):
        at = place[4 * me + slot]
        colour = 2 * half[at] + hue[at]
        first_ref[colour] = slot
        back_last_ref[slot] = colour
        at = 4 * me + slot
        colour = 2 * half[at] + hue[at]
        back_first_ref[colour] = slot
        last_ref[slot] = colour

    mine = me // 4

    def cross(p, _):
        @pl.when(2 * half[p] + hue[p] == mine)
        def _():
            source = order_ref[p] // 4
            cross_ref[p // 4] = source
            back_cross_ref[source] = p // 4

        return 0

    lax.fori_loop(0, count, cross, 0, unroll=8)
    fetch.wait()
    for i in range(out_ref.shape[0]):
        normed, _ = statistics(buffer[first_ref[i]].astype(F32))
        out_ref[i] = (normed * gain_ref[...][None]).astype(BF16)


def route(me, order, blocks, gain):
    smem = pl.BlockSpec(memory_space=pltpu.SMEM)
    vmem = pl.BlockSpec(memory_space=pltpu.VMEM)
    sizes = (4, 16, 4, 4, 16, 4)
    return pl.pallas_call(
        route_kernel,
        in_specs=[smem, smem, pl.BlockSpec(memory_space=pl.ANY), vmem],
        out_specs=[vmem] + [smem] * len(sizes),
        out_shape=[jax.ShapeDtypeStruct(blocks.shape, BF16)]
        + [jax.ShapeDtypeStruct((n,), jnp.int32) for n in sizes],
        scratch_shapes=[pltpu.SMEM(order.shape, jnp.int32)] * 3
        + [pltpu.VMEM(blocks.shape, BF16), pltpu.SemaphoreType.DMA(())],
        name="route_blocks",
    )(me[None], order, blocks, gain)


def pick_kernel(index_ref, source_ref, out_ref):
    for i in range(out_ref.shape[0]):
        out_ref[i] = source_ref[index_ref[i]]


def pick(index, source):
    return whole_call(pick_kernel, index, source, name="pick_blocks")


def statistics(values):
    centre = jnp.mean(values, axis=1, keepdims=True)
    spread = jnp.mean((values - centre) ** 2, axis=1, keepdims=True)
    inverse_std = lax.rsqrt(spread + EPSILON)
    return (values - centre) * inverse_std, inverse_std


def whole_call(kernel, index, *arrays, name):
    size = 2 * (1 + len(arrays)) * arrays[0].size
    return pl.pallas_call(
        kernel,
        in_specs=[pl.BlockSpec(memory_space=pltpu.SMEM)]
        + [pl.BlockSpec(memory_space=pltpu.VMEM)] * len(arrays),
        out_specs=pl.BlockSpec(memory_space=pltpu.VMEM),
        out_shape=jax.ShapeDtypeStruct((index.shape[0],) + arrays[0].shape[1:], BF16),
        compiler_params=pltpu.CompilerParams(vmem_limit_bytes=16 * 2**20),
        cost_estimate=pl.CostEstimate(flops=size, bytes_accessed=size, transcendentals=0),
        name=name,
    )(index, *arrays)


def norm_back_kernel(index_ref, grads_ref, rows_ref, gain_ref, out_ref):
    for i in range(out_ref.shape[0]):
        normed, inverse_std = statistics(rows_ref[i].astype(F32))
        pushed = grads_ref[index_ref[i]].astype(F32) * gain_ref[...][None]
        along = jnp.mean(pushed * normed, axis=1, keepdims=True)
        out_ref[i] = (
            inverse_std * (pushed - jnp.mean(pushed, axis=1, keepdims=True) - normed * along)
        ).astype(BF16)


def norm_back(index, grads, blocks, gain):
    return whole_call(norm_back_kernel, index, grads, blocks, gain, name="norm_back")


def assemble_kernel(parts_ref, weight_ref, gain_ref, out_ref, gain_grad_ref):
    packs, share, _ = parts_ref.shape
    heads = HEADS // packs
    width = out_ref.shape[1] // 3
    for pack in range(packs):
        cols = parts_ref[pack].astype(F32) * (1.0 / packs)
        for head in range(heads):
            for part in range(3):
                at = part * width + (pack * heads + head) * HD
                start = (3 * head + part) * HD
                out_ref[:, at : at + HD] = cols[:, start : start + HD]
    total = jnp.sum(out_ref[...] * weight_ref[...].astype(F32), axis=1, keepdims=True)
    gain_grad_ref[...] = total / gain_ref[...]


def assemble(parts, weight_rows, gain_rows):
    packs, share, per_pack = parts.shape
    vmem = pl.BlockSpec(memory_space=pltpu.VMEM)
    return pl.pallas_call(
        assemble_kernel,
        in_specs=[vmem] * 3,
        out_specs=[vmem] * 2,
        out_shape=[
            jax.ShapeDtypeStruct((share, packs * per_pack), F32),
            jax.ShapeDtypeStruct((share, 1), F32),
        ],
        compiler_params=pltpu.CompilerParams(vmem_limit_bytes=16 * 2**20),
        name="assemble",
    )(parts, weight_rows, gain_rows)


def local(loader_rows, lengths, block_order, norm_gain, qkv_weight, upstream_grad):
    seq_count = lax.axis_size(SEQ)
    pack_count = lax.axis_size(DP)
    my_index = lax.axis_index(SEQ)
    _, row_count, model_width = loader_rows.shape
    per_device = row_count // BLK
    order_row = block_order[0]
    block_total = order_row.shape[0]
    piece = BLK * per_device // seq_count
    loader_blocks = loader_rows[0].reshape(per_device, BLK, model_width)
    outgoing, _, cross, last, back_first, back_cross, back_last = route(
        my_index, order_row, loader_blocks, norm_gain
    )

    def exchange(x):
        x = x.reshape(seq_count, piece, model_width)
        return lax.all_to_all(x, SEQ, split_axis=0, concat_axis=0, tiled=True)

    up = [(i, i + 1) for i in range(seq_count - 1)]
    down = [(i + 1, i) for i in range(seq_count - 1)]

    def halo(x):
        before = lax.ppermute(x[row_count - BLK :], SEQ, up)
        after = lax.ppermute(x[:BLK], SEQ, down)
        return jnp.concatenate([before, after], axis=0)

    upstream = upstream_grad[0]
    upstream_own = upstream.T
    upstream_halo = halo(upstream).T

    spread = exchange(pick(cross, exchange(outgoing)))
    scaled = pick(last, spread.reshape(per_device, BLK, model_width)).reshape(row_count, model_width)
    scaled_halo = halo(scaled)

    def project(rows):
        return lax.dot_general(
            qkv_weight, rows, (((0,), (1,)), ((), ())), preferred_element_type=F32
        ).astype(BF16)

    qkv_own = project(scaled)
    qkv_halo = project(scaled_halo)
    image_ends = jnp.cumsum(lengths[0])
    positions = my_index * row_count - BLK + jnp.arange(row_count + 2 * BLK, dtype=jnp.int32)
    counted = jnp.sum((image_ends[None, :] <= positions[:, None]).astype(jnp.int32), axis=1)
    inside = (positions >= 0) & (positions < block_total * BLK)
    ids = jnp.where(inside, counted, -1)

    attended, grads, weight_local = attention_call(
        ids, qkv_own, qkv_halo, upstream_own, upstream_halo, scaled
    )
    weight_part = lax.psum_scatter(weight_local, DP, scatter_dimension=0, tiled=True)
    attention = attended.T[None]
    grad_cols = grads.reshape(HEADS, 3, HD, row_count)
    grad_cols = grad_cols.transpose(1, 0, 2, 3).reshape(3 * model_width, row_count)
    input_grad = lax.dot_general(
        grad_cols, qkv_weight, (((0,), (1,)), ((), ())), preferred_element_type=F32
    ).astype(BF16)
    returning = pick(back_first, input_grad.reshape(per_device, BLK, model_width))
    returned = exchange(pick(back_cross, exchange(returning)))
    loader_grad = norm_back(
        back_last, returned.reshape(per_device, BLK, model_width), loader_blocks, norm_gain
    ).reshape(1, row_count, model_width)

    share = model_width // seq_count
    per_pack = 3 * model_width // pack_count
    partial = weight_part.T.reshape(seq_count, share, per_pack)
    partial = lax.all_to_all(partial, SEQ, split_axis=0, concat_axis=0, tiled=True)
    summed = jnp.sum(partial.astype(F32), axis=0).astype(BF16)
    weight_cols = lax.all_gather(summed, DP, axis=0)
    weight_rows = lax.dynamic_slice_in_dim(qkv_weight, my_index * share, share, 0)
    gain_rows = lax.dynamic_slice_in_dim(norm_gain, my_index * share, share, 0)[:, None]
    weight_grad, gain_grad = assemble(weight_cols, weight_rows, gain_rows)
    gain_grad = gain_grad[:, 0]
    return (attention, loader_grad, weight_grad, gain_grad)


def solution(mesh):
    fine = Mesh(mesh.devices.reshape(4, 2, 4, 4), DP + SEQ)
    rows = P(DP, SEQ, None)
    return jax.shard_map(
        local,
        mesh=fine,
        in_specs=(rows, P(DP, None), P(DP, None), P(), P(), rows),
        out_specs=(rows, rows, P(SEQ, None), P(SEQ)),
        check_vma=False,
    )
```

```python
import functools

import jax
import jax.numpy as jnp
from jax import lax
from jax.experimental import pallas as pl
from jax.experimental.pallas import tpu as pltpu
from jax.sharding import Mesh
from jax.sharding import PartitionSpec as P

HEADS = 16
HD = 72
BLK = 128
PAIR = 2 * HD
BF16 = jnp.bfloat16
F32 = jnp.float32
EPSILON = 1e-06
SCORE_SCALE = HD ** (-0.5)
EXP2_SCALE = SCORE_SCALE * 1.4426950408889634
HIDDEN_BIAS = -1e30
LAG = 2
DP = ("y", "core")
SEQ = ("z", "x")


def nn(a, b):
    return lax.dot_general(a, b, (((1,), (0,)), ((), ())), preferred_element_type=F32)


def nt(a, b):
    return lax.dot_general(a, b, (((1,), (1,)), ((), ())), preferred_element_type=F32)


def attention_kernel(
    col_ref, row_ref, q_ref, k_ref, v_ref, qh_ref, kh_ref, vh_ref, g_ref, gh_ref, rows_ref,
    o_ref, d_ref, w_ref, bias_ref, o_s, d_s,
):
    blocks = q_ref.shape[1] // BLK
    rows = q_ref.shape[1]

    @pl.when(pl.program_id(0) == 0)
    def _():
        for b in range(blocks + 2):
            first, last = max(b - 1, 0), min(b + 1, blocks + 1)
            same = col_ref[b * BLK : (b + 1) * BLK, :] == row_ref[:, first * BLK : (last + 1) * BLK]
            bias_ref[b, :, : (last + 1 - first) * BLK] = jnp.where(same, 0.0, HIDDEN_BIAS)

    def operands(head):
        lo, hi = head * HD, (head + 1) * HD

        def whole(own, halo):
            mid, rim = own[...].astype(F32)[lo:hi], halo[...].astype(F32)[lo:hi]
            return jnp.concatenate([rim[:, :BLK], mid, rim[:, BLK:]], axis=1)

        q32, g32 = whole(q_ref, qh_ref), whole(g_ref, gh_ref)
        k, v = whole(k_ref, kh_ref).astype(BF16), whole(v_ref, vh_ref).astype(BF16)
        return q32, g32, q32.astype(BF16), g32.astype(BF16), k, v

    heads = [operands(head) for head in range(2)]
    for part in (1, 2, 4, 5):
        d_s[part * HD : (part + 1) * HD, :] = jnp.zeros((HD, rows), F32)

    def window(b):
        first, last = max(b - 1, 0), min(b + 1, blocks + 1)
        return first, last, slice(first * BLK, (last + 1) * BLK), slice(b * BLK, (b + 1) * BLK)

    def products(head, b):
        q32, g32, _, _, k, v = heads[head]
        _, _, near, here = window(b)
        scores = nn(q32[:, here].T.astype(BF16), k[:, near])
        grad_probs = nn(g32[:, here].T.astype(BF16), v[:, near])
        return scores, grad_probs

    def softmax(head, b, scores, grad_probs):
        weights = jnp.exp2(scores * EXP2_SCALE + bias_ref[b, :, : scores.shape[1]])
        probs = weights * (1.0 / jnp.sum(weights, axis=1, keepdims=True))
        centred = jnp.sum(probs * grad_probs, axis=1, keepdims=True)
        return probs.astype(BF16), (probs * (grad_probs - centred)).astype(BF16)

    def results(head, b, rounded, grad_scores):
        _, _, q, g, k, v = heads[head]
        first, last, near, here = window(b)
        q_at, k_at, v_at = (slice((3 * head + part) * HD, (3 * head + part + 1) * HD) for part in range(3))
        if 1 <= b <= blocks:
            own = slice((b - 1) * BLK, b * BLK)
            o_s[head * HD : (head + 1) * HD, own] = nt(v[:, near], rounded)
            d_s[q_at, own] = nt(k[:, near], grad_scores)
        k0, k1 = max(first, 1), min(last, blocks)
        seen = slice((k0 - first) * BLK, (k1 + 1 - first) * BLK)
        into = slice((k0 - 1) * BLK, k1 * BLK)
        d_s[k_at, into] += nn(q[:, here], grad_scores[:, seen])
        d_s[v_at, into] += nn(g[:, here], rounded[:, seen])

    items = [(head, b) for b in range(blocks + 2) for head in range(2)]
    scored, softened = {}, {}
    for step in range(len(items) + 2 * LAG):
        if step < len(items):
            scored[step] = products(*items[step])
        if 0 <= step - LAG < len(items):
            softened[step - LAG] = softmax(*items[step - LAG], *scored.pop(step - LAG))
        if 0 <= step - 2 * LAG:
            results(*items[step - 2 * LAG], *softened.pop(step - 2 * LAG))
    o_ref[...] = o_s[...].astype(BF16)
    for head in range(2):
        for part, factor in enumerate((SCORE_SCALE, SCORE_SCALE, None)):
            at = slice((3 * head + part) * HD, (3 * head + part + 1) * HD)
            if factor is not None:
                d_s[at, :] = d_s[at, :] * factor
    grads = d_s[...].astype(BF16)
    d_ref[...] = grads
    third = rows_ref.shape[1] // 3
    for part in range(3):
        cols = slice(part * third, (part + 1) * third)
        w_ref[:, cols] = nn(grads, rows_ref[:, cols]).astype(BF16)


def attention_call(ids, own, halo, g_own, g_halo, scaled, first_pair=0, pairs=HEADS // 2):
    rows, rim = own.shape[1], halo.shape[1]
    total, blocks = rows + rim, rows // BLK
    per_part = HEADS // 2

    def spec(width, part):
        return pl.BlockSpec((PAIR, width), lambda i: (part * per_part + first_pair + i, 0))

    return pl.pallas_call(
        attention_kernel,
        grid=(pairs,),
        in_specs=[
            pl.BlockSpec((total, 1), lambda i: (0, 0)),
            pl.BlockSpec((1, total), lambda i: (0, 0)),
            spec(rows, 0), spec(rows, 1), spec(rows, 2),
            spec(rim, 0), spec(rim, 1), spec(rim, 2),
            spec(rows, 0), spec(rim, 0),
            pl.BlockSpec(scaled.shape, lambda i: (0, 0)),
        ],
        out_specs=[
            pl.BlockSpec((PAIR, rows), lambda i: (i, 0)),
            pl.BlockSpec((3 * PAIR, rows), lambda i: (i, 0)),
            pl.BlockSpec((3 * PAIR, scaled.shape[1]), lambda i: (i, 0)),
        ],
        out_shape=[
            pltpu.HBM((pairs * PAIR, rows), BF16),
            pltpu.HBM((pairs * 3 * PAIR, rows), BF16),
            pltpu.HBM((pairs * 3 * PAIR, scaled.shape[1]), BF16),
        ],
        scratch_shapes=[
            pltpu.VMEM((blocks + 2, BLK, 3 * BLK), F32),
            pltpu.VMEM((PAIR, rows), F32),
            pltpu.VMEM((3 * PAIR, rows), F32),
        ],
        cost_estimate=pl.CostEstimate(
            flops=pairs * 2 * 16 * 12 * BLK * BLK * HD,
            bytes_accessed=pairs * PAIR * (rows * 8 + rim * 4) * 2,
            transcendentals=pairs * 2 * 16 * BLK * BLK,
        ),
        compiler_params=pltpu.CompilerParams(vmem_limit_bytes=24 * 2**20),
        name="packed_attention",
    )(ids[:, None], ids[None, :], own, own, own, halo, halo, halo, g_own, g_halo, scaled)


def route_kernel(
    me_ref, order_ref, rows_ref, gain_ref,
    out_ref, first_ref, cross_ref, last_ref, back_first_ref, back_cross_ref, back_last_ref,
    place, half, hue, buffer, arrived,
):
    fetch = pltpu.make_async_copy(rows_ref, buffer, arrived)
    fetch.start()
    me = me_ref[0]
    count = order_ref.shape[0]

    def clear(p, _):
        place[order_ref[p]] = p
        half[p] = -1
        hue[p] = -1
        return 0

    lax.fori_loop(0, count, clear, 0, unroll=8)

    def split(bits, partner, mate, seed):
        def start(i, _):
            def step(state):
                at, _ = state
                other = partner(at)
                bits[at] = 0
                bits[other] = 1
                following = mate(other)
                return following, bits[following] < 0

            at = seed(i)
            lax.while_loop(lambda state: state[1], step, (at, bits[at] < 0))
            return 0

        lax.fori_loop(0, count // 2, start, 0)

    split(half, lambda p: p ^ 1, lambda p: place[order_ref[p] ^ 1], lambda i: 2 * i)

    def same_half(p):
        return jnp.where(half[p ^ 2] == half[p], p ^ 2, p ^ 3)

    def same_half_loader(p):
        block = order_ref[p]
        near, far = place[block ^ 2], place[block ^ 3]
        return jnp.where(half[near] == half[p], near, far)

    split(hue, same_half, same_half_loader, lambda i: 4 * (i // 2) + i % 2)

    for slot in range(4):
        at = place[4 * me + slot]
        colour = 2 * half[at] + hue[at]
        first_ref[colour] = slot
        back_last_ref[slot] = colour
        at = 4 * me + slot
        colour = 2 * half[at] + hue[at]
        back_first_ref[colour] = slot
        last_ref[slot] = colour

    mine = me // 4

    def cross(p, _):
        @pl.when(2 * half[p] + hue[p] == mine)
        def _():
            source = order_ref[p] // 4
            cross_ref[p // 4] = source
            back_cross_ref[source] = p // 4

        return 0

    lax.fori_loop(0, count, cross, 0, unroll=8)
    fetch.wait()
    for i in range(out_ref.shape[0]):
        normed, _ = statistics(buffer[first_ref[i]].astype(F32))
        out_ref[i] = (normed * gain_ref[...][None]).astype(BF16)


def route(me, order, blocks, gain):
    smem = pl.BlockSpec(memory_space=pltpu.SMEM)
    vmem = pl.BlockSpec(memory_space=pltpu.VMEM)
    sizes = (4, 16, 4, 4, 16, 4)
    return pl.pallas_call(
        route_kernel,
        in_specs=[smem, smem, pl.BlockSpec(memory_space=pl.ANY), vmem],
        out_specs=[vmem] + [smem] * len(sizes),
        out_shape=[jax.ShapeDtypeStruct(blocks.shape, BF16)]
        + [jax.ShapeDtypeStruct((n,), jnp.int32) for n in sizes],
        scratch_shapes=[pltpu.SMEM(order.shape, jnp.int32)] * 3
        + [pltpu.VMEM(blocks.shape, BF16), pltpu.SemaphoreType.DMA(())],
        name="route_blocks",
    )(me[None], order, blocks, gain)


def pick_kernel(index_ref, source_ref, out_ref):
    for i in range(out_ref.shape[0]):
        out_ref[i] = source_ref[index_ref[i]]


def pick(index, source):
    return whole_call(pick_kernel, index, source, name="pick_blocks")


def statistics(values):
    centre = jnp.mean(values, axis=1, keepdims=True)
    spread = jnp.mean((values - centre) ** 2, axis=1, keepdims=True)
    inverse_std = lax.rsqrt(spread + EPSILON)
    return (values - centre) * inverse_std, inverse_std


def whole_call(kernel, index, *arrays, name):
    size = 2 * (1 + len(arrays)) * arrays[0].size
    return pl.pallas_call(
        kernel,
        in_specs=[pl.BlockSpec(memory_space=pltpu.SMEM)]
        + [pl.BlockSpec(memory_space=pltpu.VMEM)] * len(arrays),
        out_specs=pl.BlockSpec(memory_space=pltpu.VMEM),
        out_shape=jax.ShapeDtypeStruct((index.shape[0],) + arrays[0].shape[1:], BF16),
        compiler_params=pltpu.CompilerParams(vmem_limit_bytes=16 * 2**20),
        cost_estimate=pl.CostEstimate(flops=size, bytes_accessed=size, transcendentals=0),
        name=name,
    )(index, *arrays)


def norm_back_kernel(index_ref, grads_ref, rows_ref, gain_ref, out_ref):
    for i in range(out_ref.shape[0]):
        normed, inverse_std = statistics(rows_ref[i].astype(F32))
        pushed = grads_ref[index_ref[i]].astype(F32) * gain_ref[...][None]
        along = jnp.mean(pushed * normed, axis=1, keepdims=True)
        out_ref[i] = (
            inverse_std * (pushed - jnp.mean(pushed, axis=1, keepdims=True) - normed * along)
        ).astype(BF16)


def norm_back(index, grads, blocks, gain):
    return whole_call(norm_back_kernel, index, grads, blocks, gain, name="norm_back")


def assemble_kernel(parts_ref, weight_ref, gain_ref, out_ref, gain_grad_ref):
    packs, share, _ = parts_ref.shape
    heads = HEADS // packs
    width = out_ref.shape[1] // 3
    for pack in range(packs):
        cols = parts_ref[pack].astype(F32) * (1.0 / packs)
        for head in range(heads):
            for part in range(3):
                at = part * width + (pack * heads + head) * HD
                start = (3 * head + part) * HD
                out_ref[:, at : at + HD] = cols[:, start : start + HD]
    total = jnp.sum(out_ref[...] * weight_ref[...].astype(F32), axis=1, keepdims=True)
    gain_grad_ref[...] = total / gain_ref[...]


def assemble(parts, weight_rows, gain_rows):
    packs, share, per_pack = parts.shape
    vmem = pl.BlockSpec(memory_space=pltpu.VMEM)
    return pl.pallas_call(
        assemble_kernel,
        in_specs=[vmem] * 3,
        out_specs=[vmem] * 2,
        out_shape=[
            jax.ShapeDtypeStruct((share, packs * per_pack), F32),
            jax.ShapeDtypeStruct((share, 1), F32),
        ],
        compiler_params=pltpu.CompilerParams(vmem_limit_bytes=16 * 2**20),
        name="assemble",
    )(parts, weight_rows, gain_rows)


def local(loader_rows, lengths, block_order, norm_gain, qkv_weight, upstream_grad):
    seq_count = lax.axis_size(SEQ)
    pack_count = lax.axis_size(DP)
    my_index = lax.axis_index(SEQ)
    _, row_count, model_width = loader_rows.shape
    per_device = row_count // BLK
    order_row = block_order[0]
    block_total = order_row.shape[0]
    piece = BLK * per_device // seq_count
    loader_blocks = loader_rows[0].reshape(per_device, BLK, model_width)
    outgoing, _, cross, last, back_first, back_cross, back_last = route(
        my_index, order_row, loader_blocks, norm_gain
    )

    def exchange(x):
        x = x.reshape(seq_count, piece, model_width)
        return lax.all_to_all(x, SEQ, split_axis=0, concat_axis=0, tiled=True)

    up = [(i, i + 1) for i in range(seq_count - 1)]
    down = [(i + 1, i) for i in range(seq_count - 1)]

    def halo(x):
        before = lax.ppermute(x[row_count - BLK :], SEQ, up)
        after = lax.ppermute(x[:BLK], SEQ, down)
        return jnp.concatenate([before, after], axis=0)

    upstream = upstream_grad[0]
    upstream_own = upstream.T
    upstream_halo = halo(upstream).T

    spread = exchange(pick(cross, exchange(outgoing)))
    scaled = pick(last, spread.reshape(per_device, BLK, model_width)).reshape(row_count, model_width)
    scaled_halo = halo(scaled)

    def project(rows):
        return lax.dot_general(
            qkv_weight, rows, (((0,), (1,)), ((), ())), preferred_element_type=F32
        ).astype(BF16)

    qkv_own = project(scaled)
    qkv_halo = project(scaled_halo)
    image_ends = jnp.cumsum(lengths[0])
    positions = my_index * row_count - BLK + jnp.arange(row_count + 2 * BLK, dtype=jnp.int32)
    counted = jnp.sum((image_ends[None, :] <= positions[:, None]).astype(jnp.int32), axis=1)
    inside = (positions >= 0) & (positions < block_total * BLK)
    ids = jnp.where(inside, counted, -1)

    attended, grads, weight_local = attention_call(
        ids, qkv_own, qkv_halo, upstream_own, upstream_halo, scaled
    )
    weight_part = lax.psum_scatter(weight_local, DP, scatter_dimension=0, tiled=True)
    attention = attended.T[None]
    grad_cols = grads.reshape(HEADS, 3, HD, row_count)
    grad_cols = grad_cols.transpose(1, 0, 2, 3).reshape(3 * model_width, row_count)
    input_grad = lax.dot_general(
        grad_cols, qkv_weight, (((0,), (1,)), ((), ())), preferred_element_type=F32
    ).astype(BF16)
    returning = pick(back_first, input_grad.reshape(per_device, BLK, model_width))
    returned = exchange(pick(back_cross, exchange(returning)))
    loader_grad = norm_back(
        back_last, returned.reshape(per_device, BLK, model_width), loader_blocks, norm_gain
    ).reshape(1, row_count, model_width)

    share = model_width // seq_count
    per_pack = 3 * model_width // pack_count
    partial = weight_part.T.reshape(seq_count, share, per_pack)
    partial = lax.all_to_all(partial, SEQ, split_axis=0, concat_axis=0, tiled=True)
    summed = jnp.sum(partial.astype(F32), axis=0).astype(BF16)
    weight_cols = lax.all_gather(summed, DP, axis=0)
    weight_rows = lax.dynamic_slice_in_dim(qkv_weight, my_index * share, share, 0)
    gain_rows = lax.dynamic_slice_in_dim(norm_gain, my_index * share, share, 0)[:, None]
    weight_grad, gain_grad = assemble(weight_cols, weight_rows, gain_rows)
    gain_grad = gain_grad[:, 0]
    return (attention, loader_grad, weight_grad, gain_grad)


def solution(mesh):
    fine = Mesh(mesh.devices.reshape(4, 2, 4, 4), DP + SEQ)
    rows = P(DP, SEQ, None)
    return jax.shard_map(
        local,
        mesh=fine,
        in_specs=(rows, P(DP, None), P(DP, None), P(), P(), rows),
        out_specs=(rows, rows, P(SEQ, None), P(SEQ)),
        check_vma=False,
    )
```

```python
import functools

import jax
import jax.numpy as jnp
from jax import lax
from jax.experimental import pallas as pl
from jax.experimental.pallas import tpu as pltpu
from jax.sharding import Mesh
from jax.sharding import PartitionSpec as P

HEADS = 16
HD = 72
BLK = 128
PAIR = 2 * HD
BF16 = jnp.bfloat16
F32 = jnp.float32
EPSILON = 1e-06
SCORE_SCALE = HD ** (-0.5)
EXP2_SCALE = SCORE_SCALE * 1.4426950408889634
HIDDEN_BIAS = -1e30
LAG = 3
DP = ("y", "core")
SEQ = ("z", "x")


def nn(a, b):
    return lax.dot_general(a, b, (((1,), (0,)), ((), ())), preferred_element_type=F32)


def nt(a, b):
    return lax.dot_general(a, b, (((1,), (1,)), ((), ())), preferred_element_type=F32)


def attention_kernel(
    col_ref, row_ref, q_ref, k_ref, v_ref, qh_ref, kh_ref, vh_ref, g_ref, gh_ref, rows_ref,
    o_ref, d_ref, w_ref, bias_ref, o_s, d_s,
):
    blocks = q_ref.shape[1] // BLK
    rows = q_ref.shape[1]

    @pl.when(pl.program_id(0) == 0)
    def _():
        for b in range(blocks + 2):
            first, last = max(b - 1, 0), min(b + 1, blocks + 1)
            same = col_ref[b * BLK : (b + 1) * BLK, :] == row_ref[:, first * BLK : (last + 1) * BLK]
            bias_ref[b, :, : (last + 1 - first) * BLK] = jnp.where(same, 0.0, HIDDEN_BIAS)

    def operands(head):
        lo, hi = head * HD, (head + 1) * HD

        def whole(own, halo):
            mid, rim = own[...].astype(F32)[lo:hi], halo[...].astype(F32)[lo:hi]
            return jnp.concatenate([rim[:, :BLK], mid, rim[:, BLK:]], axis=1)

        q32, g32 = whole(q_ref, qh_ref), whole(g_ref, gh_ref)
        k, v = whole(k_ref, kh_ref).astype(BF16), whole(v_ref, vh_ref).astype(BF16)
        return q32, g32, q32.astype(BF16), g32.astype(BF16), k, v

    heads = [operands(head) for head in range(2)]
    for part in (1, 2, 4, 5):
        d_s[part * HD : (part + 1) * HD, :] = jnp.zeros((HD, rows), F32)

    def window(b):
        first, last = max(b - 1, 0), min(b + 1, blocks + 1)
        return first, last, slice(first * BLK, (last + 1) * BLK), slice(b * BLK, (b + 1) * BLK)

    def products(head, b):
        q32, g32, _, _, k, v = heads[head]
        _, _, near, here = window(b)
        scores = nn(q32[:, here].T.astype(BF16), k[:, near])
        grad_probs = nn(g32[:, here].T.astype(BF16), v[:, near])
        return scores, grad_probs

    def softmax(head, b, scores, grad_probs):
        weights = jnp.exp2(scores * EXP2_SCALE + bias_ref[b, :, : scores.shape[1]])
        probs = weights * (1.0 / jnp.sum(weights, axis=1, keepdims=True))
        centred = jnp.sum(probs * grad_probs, axis=1, keepdims=True)
        return probs.astype(BF16), (probs * (grad_probs - centred)).astype(BF16)

    def results(head, b, rounded, grad_scores):
        _, _, q, g, k, v = heads[head]
        first, last, near, here = window(b)
        q_at, k_at, v_at = (slice((3 * head + part) * HD, (3 * head + part + 1) * HD) for part in range(3))
        if 1 <= b <= blocks:
            own = slice((b - 1) * BLK, b * BLK)
            o_s[head * HD : (head + 1) * HD, own] = nt(v[:, near], rounded)
            d_s[q_at, own] = nt(k[:, near], grad_scores)
        k0, k1 = max(first, 1), min(last, blocks)
        seen = slice((k0 - first) * BLK, (k1 + 1 - first) * BLK)
        into = slice((k0 - 1) * BLK, k1 * BLK)
        d_s[k_at, into] += nn(q[:, here], grad_scores[:, seen])
        d_s[v_at, into] += nn(g[:, here], rounded[:, seen])

    items = [(head, b) for b in range(blocks + 2) for head in range(2)]
    scored, softened = {}, {}
    for step in range(len(items) + 2 * LAG):
        if step < len(items):
            scored[step] = products(*items[step])
        if 0 <= step - LAG < len(items):
            softened[step - LAG] = softmax(*items[step - LAG], *scored.pop(step - LAG))
        if 0 <= step - 2 * LAG:
            results(*items[step - 2 * LAG], *softened.pop(step - 2 * LAG))
    o_ref[...] = o_s[...].astype(BF16)
    for head in range(2):
        for part, factor in enumerate((SCORE_SCALE, SCORE_SCALE, None)):
            at = slice((3 * head + part) * HD, (3 * head + part + 1) * HD)
            if factor is not None:
                d_s[at, :] = d_s[at, :] * factor
    grads = d_s[...].astype(BF16)
    for part in range(3):
        first, second = part * HD, (3 + part) * HD
        both = [d_s[first : first + HD, :], d_s[second : second + HD, :]]
        d_ref[part] = jnp.concatenate(both, axis=0).astype(BF16)
    third = rows_ref.shape[1] // 3
    for part in range(3):
        cols = slice(part * third, (part + 1) * third)
        w_ref[:, cols] = nn(grads, rows_ref[:, cols]).astype(BF16)


def attention_call(ids, own, halo, g_own, g_halo, scaled, first_pair=0, pairs=HEADS // 2):
    rows, rim = own.shape[1], halo.shape[1]
    total, blocks = rows + rim, rows // BLK
    per_part = HEADS // 2

    def spec(width, part):
        return pl.BlockSpec((PAIR, width), lambda i: (part * per_part + first_pair + i, 0))

    return pl.pallas_call(
        attention_kernel,
        grid=(pairs,),
        in_specs=[
            pl.BlockSpec((total, 1), lambda i: (0, 0)),
            pl.BlockSpec((1, total), lambda i: (0, 0)),
            spec(rows, 0), spec(rows, 1), spec(rows, 2),
            spec(rim, 0), spec(rim, 1), spec(rim, 2),
            spec(rows, 0), spec(rim, 0),
            pl.BlockSpec(scaled.shape, lambda i: (0, 0)),
        ],
        out_specs=[
            pl.BlockSpec((PAIR, rows), lambda i: (i, 0)),
            pl.BlockSpec((3, PAIR, rows), lambda i: (0, i, 0)),
            pl.BlockSpec((3 * PAIR, scaled.shape[1]), lambda i: (i, 0)),
        ],
        out_shape=[
            pltpu.HBM((pairs * PAIR, rows), BF16),
            pltpu.HBM((3, pairs * PAIR, rows), BF16),
            pltpu.HBM((pairs * 3 * PAIR, scaled.shape[1]), BF16),
        ],
        scratch_shapes=[
            pltpu.VMEM((blocks + 2, BLK, 3 * BLK), F32),
            pltpu.VMEM((PAIR, rows), F32),
            pltpu.VMEM((3 * PAIR, rows), F32),
        ],
        cost_estimate=pl.CostEstimate(
            flops=pairs * 2 * 16 * 12 * BLK * BLK * HD,
            bytes_accessed=pairs * PAIR * (rows * 8 + rim * 4) * 2,
            transcendentals=pairs * 2 * 16 * BLK * BLK,
        ),
        compiler_params=pltpu.CompilerParams(vmem_limit_bytes=24 * 2**20),
        name="packed_attention",
    )(ids[:, None], ids[None, :], own, own, own, halo, halo, halo, g_own, g_halo, scaled)


def route_kernel(
    me_ref, order_ref, rows_ref, gain_ref,
    out_ref, first_ref, cross_ref, last_ref, back_first_ref, back_cross_ref, back_last_ref,
    place, half, hue, buffer, arrived,
):
    fetch = pltpu.make_async_copy(rows_ref, buffer, arrived)
    fetch.start()
    me = me_ref[0]
    count = order_ref.shape[0]

    def clear(p, _):
        place[order_ref[p]] = p
        half[p] = -1
        hue[p] = -1
        return 0

    lax.fori_loop(0, count, clear, 0, unroll=8)

    def split(bits, partner, mate, seed):
        def start(i, _):
            def step(state):
                at, _ = state
                other = partner(at)
                bits[at] = 0
                bits[other] = 1
                following = mate(other)
                return following, bits[following] < 0

            at = seed(i)
            lax.while_loop(lambda state: state[1], step, (at, bits[at] < 0))
            return 0

        lax.fori_loop(0, count // 2, start, 0)

    split(half, lambda p: p ^ 1, lambda p: place[order_ref[p] ^ 1], lambda i: 2 * i)

    def same_half(p):
        return jnp.where(half[p ^ 2] == half[p], p ^ 2, p ^ 3)

    def same_half_loader(p):
        block = order_ref[p]
        near, far = place[block ^ 2], place[block ^ 3]
        return jnp.where(half[near] == half[p], near, far)

    split(hue, same_half, same_half_loader, lambda i: 4 * (i // 2) + i % 2)

    for slot in range(4):
        at = place[4 * me + slot]
        colour = 2 * half[at] + hue[at]
        first_ref[colour] = slot
        back_last_ref[slot] = colour
        at = 4 * me + slot
        colour = 2 * half[at] + hue[at]
        back_first_ref[colour] = slot
        last_ref[slot] = colour

    mine = me // 4

    def cross(p, _):
        @pl.when(2 * half[p] + hue[p] == mine)
        def _():
            source = order_ref[p] // 4
            cross_ref[p // 4] = source
            back_cross_ref[source] = p // 4

        return 0

    lax.fori_loop(0, count, cross, 0, unroll=8)
    fetch.wait()
    for i in range(out_ref.shape[0]):
        normed, _ = statistics(buffer[first_ref[i]].astype(F32))
        out_ref[i] = (normed * gain_ref[...][None]).astype(BF16)


def route(me, order, blocks, gain):
    smem = pl.BlockSpec(memory_space=pltpu.SMEM)
    vmem = pl.BlockSpec(memory_space=pltpu.VMEM)
    sizes = (4, 16, 4, 4, 16, 4)
    return pl.pallas_call(
        route_kernel,
        in_specs=[smem, smem, pl.BlockSpec(memory_space=pl.ANY), vmem],
        out_specs=[vmem] + [smem] * len(sizes),
        out_shape=[jax.ShapeDtypeStruct(blocks.shape, BF16)]
        + [jax.ShapeDtypeStruct((n,), jnp.int32) for n in sizes],
        scratch_shapes=[pltpu.SMEM(order.shape, jnp.int32)] * 3
        + [pltpu.VMEM(blocks.shape, BF16), pltpu.SemaphoreType.DMA(())],
        name="route_blocks",
    )(me[None], order, blocks, gain)


def pick_kernel(index_ref, source_ref, out_ref):
    for i in range(out_ref.shape[0]):
        out_ref[i] = source_ref[index_ref[i]]


def pick(index, source):
    return whole_call(pick_kernel, index, source, name="pick_blocks")


def statistics(values):
    centre = jnp.mean(values, axis=1, keepdims=True)
    spread = jnp.mean((values - centre) ** 2, axis=1, keepdims=True)
    inverse_std = lax.rsqrt(spread + EPSILON)
    return (values - centre) * inverse_std, inverse_std


def whole_call(kernel, index, *arrays, name):
    size = 2 * (1 + len(arrays)) * arrays[0].size
    return pl.pallas_call(
        kernel,
        in_specs=[pl.BlockSpec(memory_space=pltpu.SMEM)]
        + [pl.BlockSpec(memory_space=pltpu.VMEM)] * len(arrays),
        out_specs=pl.BlockSpec(memory_space=pltpu.VMEM),
        out_shape=jax.ShapeDtypeStruct((index.shape[0],) + arrays[0].shape[1:], BF16),
        compiler_params=pltpu.CompilerParams(vmem_limit_bytes=16 * 2**20),
        cost_estimate=pl.CostEstimate(flops=size, bytes_accessed=size, transcendentals=0),
        name=name,
    )(index, *arrays)


def norm_back_kernel(index_ref, grads_ref, rows_ref, gain_ref, out_ref):
    for i in range(out_ref.shape[0]):
        normed, inverse_std = statistics(rows_ref[i].astype(F32))
        pushed = grads_ref[index_ref[i]].astype(F32) * gain_ref[...][None]
        along = jnp.mean(pushed * normed, axis=1, keepdims=True)
        out_ref[i] = (
            inverse_std * (pushed - jnp.mean(pushed, axis=1, keepdims=True) - normed * along)
        ).astype(BF16)


def norm_back(index, grads, blocks, gain):
    return whole_call(norm_back_kernel, index, grads, blocks, gain, name="norm_back")


def assemble_kernel(parts_ref, weight_ref, gain_ref, out_ref, gain_grad_ref):
    packs, share, _ = parts_ref.shape
    heads = HEADS // packs
    width = out_ref.shape[1] // 3
    for pack in range(packs):
        cols = parts_ref[pack].astype(F32) * (1.0 / packs)
        for head in range(heads):
            for part in range(3):
                at = part * width + (pack * heads + head) * HD
                start = (3 * head + part) * HD
                out_ref[:, at : at + HD] = cols[:, start : start + HD]
    total = jnp.sum(out_ref[...] * weight_ref[...].astype(F32), axis=1, keepdims=True)
    gain_grad_ref[...] = total / gain_ref[...]


def assemble(parts, weight_rows, gain_rows):
    packs, share, per_pack = parts.shape
    vmem = pl.BlockSpec(memory_space=pltpu.VMEM)
    return pl.pallas_call(
        assemble_kernel,
        in_specs=[vmem] * 3,
        out_specs=[vmem] * 2,
        out_shape=[
            jax.ShapeDtypeStruct((share, packs * per_pack), F32),
            jax.ShapeDtypeStruct((share, 1), F32),
        ],
        compiler_params=pltpu.CompilerParams(vmem_limit_bytes=16 * 2**20),
        name="assemble",
    )(parts, weight_rows, gain_rows)


def local(loader_rows, lengths, block_order, norm_gain, qkv_weight, upstream_grad):
    seq_count = lax.axis_size(SEQ)
    pack_count = lax.axis_size(DP)
    my_index = lax.axis_index(SEQ)
    _, row_count, model_width = loader_rows.shape
    per_device = row_count // BLK
    order_row = block_order[0]
    block_total = order_row.shape[0]
    piece = BLK * per_device // seq_count
    loader_blocks = loader_rows[0].reshape(per_device, BLK, model_width)
    outgoing, _, cross, last, back_first, back_cross, back_last = route(
        my_index, order_row, loader_blocks, norm_gain
    )

    def exchange(x):
        x = x.reshape(seq_count, piece, model_width)
        return lax.all_to_all(x, SEQ, split_axis=0, concat_axis=0, tiled=True)

    up = [(i, i + 1) for i in range(seq_count - 1)]
    down = [(i + 1, i) for i in range(seq_count - 1)]

    def halo(x):
        before = lax.ppermute(x[row_count - BLK :], SEQ, up)
        after = lax.ppermute(x[:BLK], SEQ, down)
        return jnp.concatenate([before, after], axis=0)

    upstream = upstream_grad[0]
    upstream_own = upstream.T
    upstream_halo = halo(upstream).T

    spread = exchange(pick(cross, exchange(outgoing)))
    scaled = pick(last, spread.reshape(per_device, BLK, model_width)).reshape(row_count, model_width)
    scaled_halo = halo(scaled)

    def project(rows):
        return lax.dot_general(
            qkv_weight, rows, (((0,), (1,)), ((), ())), preferred_element_type=F32
        ).astype(BF16)

    qkv_own = project(scaled)
    qkv_halo = project(scaled_halo)
    image_ends = jnp.cumsum(lengths[0])
    positions = my_index * row_count - BLK + jnp.arange(row_count + 2 * BLK, dtype=jnp.int32)
    counted = jnp.sum((image_ends[None, :] <= positions[:, None]).astype(jnp.int32), axis=1)
    inside = (positions >= 0) & (positions < block_total * BLK)
    ids = jnp.where(inside, counted, -1)

    attended, grads, weight_local = attention_call(
        ids, qkv_own, qkv_halo, upstream_own, upstream_halo, scaled
    )
    weight_part = lax.psum_scatter(weight_local, DP, scatter_dimension=0, tiled=True)
    attention = attended.T[None]
    grad_cols = grads.reshape(3 * model_width, row_count)
    input_grad = lax.dot_general(
        grad_cols, qkv_weight, (((0,), (1,)), ((), ())), preferred_element_type=F32
    ).astype(BF16)
    returning = pick(back_first, input_grad.reshape(per_device, BLK, model_width))
    returned = exchange(pick(back_cross, exchange(returning)))
    loader_grad = norm_back(
        back_last, returned.reshape(per_device, BLK, model_width), loader_blocks, norm_gain
    ).reshape(1, row_count, model_width)

    share = model_width // seq_count
    per_pack = 3 * model_width // pack_count
    partial = weight_part.T.reshape(seq_count, share, per_pack)
    partial = lax.all_to_all(partial, SEQ, split_axis=0, concat_axis=0, tiled=True)
    summed = jnp.sum(partial.astype(F32), axis=0).astype(BF16)
    weight_cols = lax.all_gather(summed, DP, axis=0)
    weight_rows = lax.dynamic_slice_in_dim(qkv_weight, my_index * share, share, 0)
    gain_rows = lax.dynamic_slice_in_dim(norm_gain, my_index * share, share, 0)[:, None]
    weight_grad, gain_grad = assemble(weight_cols, weight_rows, gain_rows)
    gain_grad = gain_grad[:, 0]
    return (attention, loader_grad, weight_grad, gain_grad)


def solution(mesh):
    fine = Mesh(mesh.devices.reshape(4, 2, 4, 4), DP + SEQ)
    rows = P(DP, SEQ, None)
    return jax.shard_map(
        local,
        mesh=fine,
        in_specs=(rows, P(DP, None), P(DP, None), P(), P(), rows),
        out_specs=(rows, rows, P(SEQ, None), P(SEQ)),
        check_vma=False,
    )
```
